32 devices in a mesh: groups: 2 (over y), edge: 4 (over z), expert: 2 (over x), sys: 2 (over core).
Axes of the slice: x: 2, y: 2, z: 4, core: 2. Of those that a mesh axis runs over, the one named last changes fastest.
Arguments:
- edge_inputs: bfloat16 [8, 1792, 1280], P(('groups', 'expert', 'sys'), 'edge'), parts along dimension 0, may hold values from -6 to 6
- out_grad: bfloat16 [8, 1792, 1152], P(('groups', 'expert', 'sys'), 'edge'), parts along dimension 0, may hold values from -6 to 6
- expert_weights: bfloat16 [32, 1280, 1152], P('expert', 'edge'), may hold values from -0.15625 to 0.15625
- coef_table: float32 [16, 32], replicated, may hold values from 0.05 to 0.5
- system_kind: int32 [8], P('groups'), parts along dimension 0, may hold values from 0 to 15
- edge_counts: int32 [8], P('groups'), parts along dimension 0, may hold values from 896 to 1792, as said below
Outputs:
- input_grad: bfloat16 [8, 1792, 1280], P(('groups', 'expert', 'sys'), 'edge'), parts along dimension 0
- weight_grad: bfloat16 [64, 1280, 1152], P(('groups', 'expert'), 'edge'), parts along dimension 0
The draws below stay inside these ranges and needn't reach their ends.
There are 2 independent parts, one for each index of `groups`. The reference program is written for one: setup_inputs(seed, part) draws one part's arguments, and reference() takes and returns one part's arrays. A program takes and returns all parts, laid end to end along the dimension named above; an argument that names none is the same for every part. Nothing has to cross between parts.
Inputs may be any that keep to these rules, and one draw needn't show every extreme that they name: `edge_counts`: the live edges of a system are its first ones. One system has all 1792 slots live and another exactly half of them.
All inputs are finite; a program needn't handle non-finite values.
Results may differ from the reference program's by a relative error of at most 0.018.
Values may be sent and summed in bfloat16 or wider, within the bound.
No kernel may reach another device: no remote copies, remote signals or barrier semaphores. Data moves between devices by JAX's collectives and lax.ppermute only.
A program may use at most 128 MiB of HBM per device.

```python
import math
import jax
import jax.numpy as jnp
from jax import lax

DIN = 1280
DOUT = 1152
EXPERTS = 32
KINDS = 16
EDGE_DEV = 448
SYSTEMS = 4
EDGES = 1792
N_EDGE = 4
N_EXPERT = 2


def draw_edge_counts(key, part):
    key_counts, key_order = jax.random.split(jax.random.fold_in(key, 7), 2)
    half_edges = EDGES // 2
    counts = jax.random.randint(key_counts, (SYSTEMS,), half_edges, EDGES + 1)
    order = jax.random.permutation(key_order, SYSTEMS)
    counts = jnp.where(order == 0, EDGES, counts)
    counts = jnp.where(order == 1, half_edges, counts)
    return counts.astype(jnp.int32)


def plant(result, stream_key, smallest, high):
    extent = result.shape
    spot = [jax.random.randint(jax.random.fold_in(stream_key, axis), (), 0, extent[axis]) for axis in range(len(extent))]
    result = result.at[tuple(spot)].set(smallest)
    longest = extent.index(max(extent))
    spot[longest] = (spot[longest] + 1) % extent[longest]
    return result.at[tuple(spot)].set(high)


def steps_of(stream_key, extent, shards, smallest, high):
    gain, own = 1.0, jax.random.fold_in(stream_key, 6)
    for dim, parts in shards:
        heights = jnp.exp(jax.random.uniform(jax.random.fold_in(own, dim), (parts,), jnp.float32, smallest / len(shards), high / len(shards)))
        gain = gain * jnp.repeat(heights, extent[dim] // parts).reshape([-1 if axis == dim else 1 for axis in range(len(extent))])
    return gain


def scatter_about(own_key, dims, scale, bound, cuts=(), kind=jnp.bfloat16):
    loudness = steps_of(own_key, dims, cuts, -0.22, 0.18) if cuts else 1.0
    result = jax.random.normal(own_key, dims, jnp.float32) * scale * loudness
    return jnp.minimum(jnp.maximum(result, -bound), bound).astype(kind)


def setup_inputs(seed: int = 0, part: int = 0) -> dict:
    splits = jax.random.split(jax.random.key(seed), 7)
    part_splits = jax.random.split(jax.random.fold_in(splits[6], part), 7)
    return {
        "edge_inputs": scatter_about(part_splits[0], (SYSTEMS, EDGES, DIN), 1.0, 6.0, ((0, 4), (1, 4))),
        "out_grad": scatter_about(part_splits[1], (SYSTEMS, EDGES, DOUT), 1.0, 6.0, ((0, 4), (1, 4))),
        "expert_weights": scatter_about(splits[2], (EXPERTS, DIN, DOUT), DIN ** -0.5, 0.15625, ((0, 2), (1, 4))),
        "coef_table": jnp.clip(jnp.exp(jax.random.uniform(splits[3], (KINDS, EXPERTS), jnp.float32, math.log(0.05), math.log(0.5))), 0.05, 0.5),
        "system_kind": plant(jax.random.randint(part_splits[4], (SYSTEMS,), 0, KINDS), jax.random.fold_in(part_splits[4], 1), 0, KINDS - 1).astype(jnp.int32),
        "edge_counts": draw_edge_counts(jax.random.fold_in(jax.random.fold_in(splits[6], part), 71), part),
    }


def reference(edge_inputs, out_grad, expert_weights, coef_table, system_kind, edge_counts):
    highest = lax.Precision.HIGHEST
    onehot = (system_kind[:, None] == jnp.arange(KINDS, dtype=jnp.int32)[None, :]).astype(jnp.float32)
    coeffs = jnp.dot(onehot, coef_table, precision=highest)
    live = jnp.arange(EDGES, dtype=jnp.int32)[None, :] < edge_counts[:, None]
    masked_grad = jnp.where(live[:, :, None], out_grad, jnp.zeros((), out_grad.dtype))
    per_block = EXPERTS // N_EXPERT
    weights_float = expert_weights.astype(jnp.float32).reshape(N_EXPERT, per_block, DIN, DOUT)

    def merge_one(row):
        scaled = row.reshape(N_EXPERT, per_block)
        partials = jnp.einsum('be,berd->brd', scaled, weights_float, precision=highest).astype(jnp.bfloat16)
        return lax.optimization_barrier(jnp.sum(partials.astype(jnp.float32), axis=0)).astype(jnp.bfloat16)
    merged = lax.map(merge_one, coeffs)

    def input_one(pair):
        grad_rows, merged_one = pair
        product = jnp.dot(grad_rows.astype(jnp.float32), merged_one.astype(jnp.float32).T, precision=highest)
        return product.astype(jnp.bfloat16)
    input_grad = lax.map(input_one, (masked_grad, merged))

    def system_one(pair):
        feat_rows, grad_rows = pair
        feat_blocks = feat_rows.astype(jnp.float32).reshape(N_EDGE, EDGE_DEV, DIN)
        grad_blocks = grad_rows.astype(jnp.float32).reshape(N_EDGE, EDGE_DEV, DOUT)
        block_grads = jnp.einsum('bnd,bnk->bdk', feat_blocks, grad_blocks, precision=highest).astype(jnp.bfloat16)
        return lax.optimization_barrier(jnp.sum(block_grads.astype(jnp.float32), axis=0)).astype(jnp.bfloat16)
    system_grads = lax.map(system_one, (edge_inputs, masked_grad))
    summed = jnp.einsum('se,sdk->edk', coeffs, system_grads.astype(jnp.float32), precision=highest)
    weight_grad = (summed * (1.0 / math.sqrt(EDGES))).astype(jnp.bfloat16)
    return (input_grad, weight_grad)
```

```python
import functools
import math

import jax
import jax.numpy as jnp
from jax import lax
from jax.experimental import pallas as pl
from jax.experimental.pallas import tpu as pltpu
from jax.sharding import PartitionSpec as P

LAG = 3
MERGED_AT = (6, 8)


def plan(size, chunks, lag, merged_at):
    sums = {}
    rows = {(z, z, h): merged_at[min(h, len(merged_at) - 1)] + 2 * max(0, h - 1) for z in range(size) for h in range(chunks)}
    for h in range(chunks):
        for b in range(size):
            if b > 0:
                sums[(0, 1, b, h)] = 0
            if b < size - 1:
                sums[(size - 1, -1, b, h)] = 0
    sent = set()
    steps = []
    total = 2 * chunks * size * (size - 1)
    while len(sent) < total:
        at = len(steps)
        step = []
        for low in range(at % 2, size - 1, 2):
            for source, way in ((low, 1), (low + 1, -1)):
                target = source + way
                ready = []
                for h in range(chunks):
                    for b in range(size):
                        ahead = (b - target) * way
                        if ahead >= 0:
                            key = ("S", source, way, b, h)
                            if key not in sent and sums.get((source, way, b, h), at + 1) <= at:
                                ready.append(((0, -ahead, h), key, b, h))
                        if (source - b) * way >= 0:
                            key = ("M", source, way, b, h)
                            left = size - 1 - target if way == 1 else target
                            if key not in sent and rows.get((source, b, h), at + 1) <= at:
                                ready.append(((1, -left, h), key, b, h))
                if ready:
                    _, key, b, h = min(ready)
                    sent.add(key)
                    step.append((source, target, key[0], b, h))
        for source, target, kind, b, h in step:
            if kind == "M":
                rows[(target, b, h)] = at + lag
            elif b != target:
                sums[(target, target - source, b, h)] = at + lag
        steps.append(step)
    return steps


def merge_kernel(count, coeff_ref, weights_ref, *out_refs):
    experts, rows, _ = weights_ref.shape
    for start in range(0, rows, 16):
        span = pl.ds(start, 16)
        totals = [None] * count
        for e in range(experts):
            weight = weights_ref[e, span, :].astype(jnp.float32)
            for k in range(count):
                term = coeff_ref[k, e] * weight
                totals[k] = term if totals[k] is None else totals[k] + term
        for k in range(count):
            out_refs[k][span, :] = totals[k].astype(jnp.bfloat16)


def merge_part(coeffs, weights, first, rows, tile):
    count, experts = coeffs.shape
    width = weights.shape[2]
    return pl.pallas_call(
        functools.partial(merge_kernel, count),
        grid=(rows // tile,),
        in_specs=[
            pl.BlockSpec(memory_space=pltpu.SMEM),
            pl.BlockSpec((experts, tile, width), lambda i: (0, first // tile + i, 0)),
        ],
        out_specs=[pl.BlockSpec((tile, width), lambda i: (i, 0))] * count,
        out_shape=[jax.ShapeDtypeStruct((rows, width), jnp.bfloat16)] * count,
        compiler_params=pltpu.CompilerParams(vmem_limit_bytes=16 << 20),
        cost_estimate=pl.CostEstimate(
            flops=2 * count * experts * rows * width, bytes_accessed=2 * experts * rows * width, transcendentals=0
        ),
        name="merge",
    )(coeffs, weights)


def live_rows(grad_ref, live_ref):
    at = lax.broadcasted_iota(jnp.int32, grad_ref.shape, 0)
    return jnp.where(at < live_ref[0], grad_ref[...], jnp.zeros((), grad_ref.dtype))


def outer_kernel(live_ref, features_ref, grad_ref, out_ref, masked):
    @pl.when(pl.program_id(0) == 0)
    def _():
        masked[...] = live_rows(grad_ref, live_ref)

    out_ref[...] = lax.dot_general(
        features_ref[...], masked[...], (((0,), (0,)), ((), ())), preferred_element_type=jnp.float32
    ).astype(out_ref.dtype)


def outer_products(live, features, grad):
    edges, width_in = features.shape
    width = grad.shape[1]
    tile = 256 if width_in % 256 == 0 else width_in
    return pl.pallas_call(
        outer_kernel,
        grid=(width_in // tile,),
        in_specs=[
            pl.BlockSpec(memory_space=pltpu.SMEM),
            pl.BlockSpec((edges, tile), lambda i: (0, i)),
            pl.BlockSpec((edges, width), lambda i: (0, 0)),
        ],
        out_specs=pl.BlockSpec((tile, width), lambda i: (i, 0)),
        out_shape=jax.ShapeDtypeStruct((width_in, width), jnp.bfloat16),
        scratch_shapes=[pltpu.VMEM((edges, width), jnp.bfloat16)],
        compiler_params=pltpu.CompilerParams(vmem_limit_bytes=16 << 20),
        cost_estimate=pl.CostEstimate(
            flops=2 * edges * width_in * width,
            bytes_accessed=2 * (edges * width_in + edges * width + width_in * width),
            transcendentals=0,
        ),
        name="outer",
    )(live, features, grad)


def input_kernel(live_ref, grad_ref, rows_ref, out_ref, masked):
    @pl.when(pl.program_id(0) == 0)
    def _():
        masked[...] = live_rows(grad_ref, live_ref)

    out_ref[...] = lax.dot_general(
        masked[...], rows_ref[...], (((1,), (1,)), ((), ())), preferred_element_type=jnp.float32
    ).astype(out_ref.dtype)


def input_product(live, grad, merged):
    edges, width = grad.shape
    width_in = merged.shape[0]
    tile = 256 if width_in % 256 == 0 else width_in
    return pl.pallas_call(
        input_kernel,
        grid=(width_in // tile,),
        in_specs=[
            pl.BlockSpec(memory_space=pltpu.SMEM),
            pl.BlockSpec((edges, width), lambda i: (0, 0)),
            pl.BlockSpec((tile, width), lambda i: (i, 0)),
        ],
        out_specs=pl.BlockSpec((edges, tile), lambda i: (0, i)),
        out_shape=jax.ShapeDtypeStruct((edges, width_in), jnp.bfloat16),
        scratch_shapes=[pltpu.VMEM((edges, width), jnp.bfloat16)],
        compiler_params=pltpu.CompilerParams(vmem_limit_bytes=16 << 20),
        cost_estimate=pl.CostEstimate(
            flops=2 * edges * width_in * width,
            bytes_accessed=2 * (edges * width_in + edges * width + width_in * width),
            transcendentals=0,
        ),
        name="input_product",
    )(live, grad, merged)


def spread_kernel(count, groups, mix_ref, *refs):
    out_ref = refs[-1]
    experts, tile, width = out_ref.shape
    rows = jnp.concatenate([ref[...] for ref in refs[:count]], axis=0)
    rows = jnp.concatenate([rows, rows], axis=0)
    span = experts // groups
    for g in range(groups):
        part = jnp.dot(
            mix_ref[pl.ds(g * span * tile, span * tile), :], rows, preferred_element_type=jnp.float32
        )
        out_ref[pl.ds(g * span, span)] = part.astype(out_ref.dtype).reshape(span, tile, width)


def spread(mix, pieces, previous, experts, first, rows_all, tile):
    rows, width = pieces[0].shape
    count = len(pieces)
    groups = 4 if experts % 4 == 0 else 1
    specs = [pl.BlockSpec(mix.shape, lambda i: (0, 0))]
    specs += [pl.BlockSpec((tile, width), lambda i: (i, 0))] * count
    operands = [mix, *pieces]
    aliases = {}
    if previous is not None:
        specs.append(pl.BlockSpec(memory_space=pl.ANY))
        operands.append(previous)
        aliases = {len(operands) - 1: 0}
    return pl.pallas_call(
        functools.partial(spread_kernel, count, groups),
        grid=(rows // tile,),
        in_specs=specs,
        out_specs=pl.BlockSpec((experts, tile, width), lambda i: (0, first // tile + i, 0)),
        out_shape=jax.ShapeDtypeStruct((experts, rows_all, width), jnp.bfloat16),
        input_output_aliases=aliases,
        compiler_params=pltpu.CompilerParams(vmem_limit_bytes=24 << 20),
        cost_estimate=pl.CostEstimate(
            flops=2 * mix.size * rows // tile * width, bytes_accessed=2 * experts * rows * width, transcendentals=0
        ),
        name="spread",
    )(*operands)


def body(edge_inputs, out_grad, expert_weights, coef_table, system_kind, edge_counts):
    highest = lax.Precision.HIGHEST
    edge_size = lax.axis_size("edge")
    expert_size = lax.axis_size("expert")
    sys_size = lax.axis_size("sys")
    edge_at = lax.axis_index("edge")
    expert_at = lax.axis_index("expert")
    sys_at = lax.axis_index("sys")
    systems = system_kind.shape[0]
    kinds = coef_table.shape[0]
    exp_local, row_count, width_out = expert_weights.shape
    edge_rows = out_grad.shape[1]
    chunks = 2 if row_count % 32 == 0 else 1
    rows = row_count // chunks
    tile = 32 if rows % 32 == 0 else 16
    features, grad = edge_inputs[0], out_grad[0]

    own_system = expert_at * sys_size + sys_at
    picked = jnp.arange(systems, dtype=jnp.int32) == own_system
    own_count = jnp.sum(jnp.where(picked, edge_counts, 0))
    live = jnp.reshape(own_count - edge_at * edge_rows, (1,)).astype(jnp.int32)

    onehot = (system_kind[:, None] == jnp.arange(kinds, dtype=jnp.int32)[None, :]).astype(jnp.float32)
    coeffs = jnp.dot(onehot, coef_table, precision=highest)
    own_coeffs = lax.dynamic_slice_in_dim(coeffs, expert_at * exp_local, exp_local, 1)
    by_expert = own_coeffs.reshape(expert_size, sys_size, exp_local)
    same_sys = lax.dynamic_slice_in_dim(by_expert, sys_at, 1, 1)[:, 0, :]
    ahead = jnp.roll(same_sys, -expert_at, axis=0)

    products = outer_products(live, features, grad).reshape(edge_size * chunks, rows, width_out)

    merged = []
    for h in range(chunks):
        parts = merge_part(ahead, expert_weights, h * rows, rows, tile)
        total = parts[0].astype(jnp.float32)
        for k in range(1, expert_size):
            shift = [(i, (i + k) % expert_size) for i in range(expert_size)]
            total = total + lax.ppermute(parts[k], "expert", shift).astype(jnp.float32)
        merged.append(total.astype(jnp.bfloat16))

    steps = plan(edge_size, chunks, LAG, MERGED_AT)
    arrived = {}
    got = {}

    def choose(wanted, start):
        value = start
        for key, devices in wanted.items():
            array = merged[key[1]] if key[0] == "own" else got[key[1]]
            if value is None:
                value = array
                continue
            here = functools.reduce(jnp.logical_or, [edge_at == z for z in devices])
            value = jnp.where(here, array, value)
        return value

    for at, step in enumerate(steps):
        if not step:
            continue
        index = [0] * edge_size
        plain, added, moved = set(), {}, {}
        for source, target, kind, b, h in step:
            way = target - source
            if kind == "S":
                index[source] = b * chunks + h
                before = arrived.get((source, kind, way, b, h))
                if before is None:
                    plain.add(source)
                else:
                    added.setdefault(("step", before), []).append(source)
            elif b == source:
                moved.setdefault(("own", h), []).append(source)
            else:
                moved.setdefault(("step", arrived[(source, kind, way, b, h)]), []).append(source)
        message = None
        if plain or added:
            where = jnp.asarray(index, jnp.int32)[edge_at]
            message = lax.dynamic_index_in_dim(products, where, 0, keepdims=False)
            if added:
                extra = choose(added, None)
                total = (message.astype(jnp.float32) + extra.astype(jnp.float32)).astype(jnp.bfloat16)
                if plain:
                    here = functools.reduce(jnp.logical_or, [edge_at == z for z in plain])
                    message = jnp.where(here, message, total)
                else:
                    message = total
        message = choose(moved, message)
        got[at] = lax.ppermute(message, "edge", [(source, target) for source, target, *_ in step])
        for source, target, kind, b, h in step:
            arrived[(target, kind, target - source, b, h)] = at

    offsets = [(k, l) for k in range(expert_size) for l in range(sys_size)]
    result = None
    own_experts = coeffs[:, :] if expert_size == 1 else own_coeffs
    scale_factor = 1.0 / math.sqrt(edge_rows * edge_size)
    slots = []
    for l in range(sys_size):
        for k in range(expert_size):
            system = ((expert_at - k) % expert_size) * sys_size + (sys_at - l) % sys_size
            slots.append(lax.dynamic_index_in_dim(own_experts, system, 0, keepdims=False))
    weights = jnp.stack(slots, axis=1) * scale_factor
    high = weights.astype(jnp.bfloat16)
    low = (weights - high.astype(jnp.float32)).astype(jnp.bfloat16)
    eye = jnp.eye(tile, dtype=jnp.bfloat16)
    mix = jnp.concatenate(
        [
            (part[:, None, :, None] * eye[None, :, None, :]).reshape(exp_local * tile, len(offsets) * tile)
            for part in (high, low)
        ],
        axis=1,
    )
    for h in range(chunks):
        total = lax.dynamic_index_in_dim(products, edge_at * chunks + h, 0, keepdims=False).astype(jnp.float32)
        for way in (1, -1):
            wanted = {}
            for z in range(edge_size):
                before = arrived.get((z, "S", way, z, h))
                if before is not None:
                    wanted.setdefault(before, []).append(z)
            for before, devices in wanted.items():
                here = functools.reduce(jnp.logical_or, [edge_at == z for z in devices])
                total = total + jnp.where(here, got[before].astype(jnp.float32), 0.0)
        own_rows = total.astype(jnp.bfloat16)
        column = [own_rows]
        for k in range(1, expert_size):
            shift = [(i, (i + k) % expert_size) for i in range(expert_size)]
            column.append(lax.ppermute(own_rows, "expert", shift))
        pieces = list(column)
        for l in range(1, sys_size):
            shift = [(i, (i + l) % sys_size) for i in range(sys_size)]
            pieces += [lax.ppermute(piece, "sys", shift) for piece in column]
        result = spread(mix, pieces, result, exp_local, h * rows, row_count, tile)

    blocks = []
    for b in range(edge_size):
        for h in range(chunks):
            wanted = {("own", h): [b]}
            for z in range(edge_size):
                if z != b:
                    way = 1 if z > b else -1
                    wanted.setdefault(("step", arrived[(z, "M", way, b, h)]), []).append(z)
            blocks.append(choose(wanted, None))
    input_grad = input_product(live, grad, jnp.concatenate(blocks, axis=0))
    return (input_grad[None], result)


def solution(mesh):
    return jax.shard_map(
        body,
        mesh=mesh,
        in_specs=(
            P(("groups", "expert", "sys"), "edge", None),
            P(("groups", "expert", "sys"), "edge", None),
            P("expert", "edge", None),
            P(),
            P("groups"),
            P("groups"),
        ),
        out_specs=(
            P(("groups", "expert", "sys"), "edge", None),
            P(("groups", "expert"), "edge", None),
        ),
        check_vma=False,
    )
```

```python
import functools
import math

import jax
import jax.numpy as jnp
from jax import lax
from jax.experimental import pallas as pl
from jax.experimental.pallas import tpu as pltpu
from jax.sharding import PartitionSpec as P

LAG = 3
MERGED_AT = (6, 8)


def plan(size, chunks, lag, merged_at):
    sums = {}
    rows = {(z, z, h): merged_at[min(h, len(merged_at) - 1)] + 2 * max(0, h - 1) for z in range(size) for h in range(chunks)}
    for h in range(chunks):
        for b in range(size):
            if b > 0:
                sums[(0, 1, b, h)] = 0
            if b < size - 1:
                sums[(size - 1, -1, b, h)] = 0
    sent = set()
    steps = []
    total = 2 * chunks * size * (size - 1)
    while len(sent) < total:
        at = len(steps)
        step = []
        for low in range(at % 2, size - 1, 2):
            for source, way in ((low, 1), (low + 1, -1)):
                target = source + way
                ready = []
                for h in range(chunks):
                    for b in range(size):
                        ahead = (b - target) * way
                        if ahead >= 0:
                            key = ("S", source, way, b, h)
                            if key not in sent and sums.get((source, way, b, h), at + 1) <= at:
                                ready.append(((0, -ahead, h), key, b, h))
                        if (source - b) * way >= 0:
                            key = ("M", source, way, b, h)
                            left = size - 1 - target if way == 1 else target
                            if key not in sent and rows.get((source, b, h), at + 1) <= at:
                                ready.append(((1, -left, h), key, b, h))
                if ready:
                    _, key, b, h = min(ready)
                    sent.add(key)
                    step.append((source, target, key[0], b, h))
        for source, target, kind, b, h in step:
            if kind == "M":
                rows[(target, b, h)] = at + lag
            elif b != target:
                sums[(target, target - source, b, h)] = at + lag
        steps.append(step)
    return steps


def at_device(values):
    place = lax.axis_index("edge")
    result = jnp.int32(values[0])
    for z in range(1, len(values)):
        if values[z] != values[z - 1]:
            result = jnp.where(place >= z, jnp.int32(values[z]), result)
    return result


def coefficient(table_ref, kind_ref, system, expert):
    return table_ref[kind_ref[system], expert]


def merge_kernel(expert_size, sys_size, first, tile, table_ref, kind_ref, weights_ref, *out_refs):
    experts, _, width = weights_ref.shape
    rows = out_refs[0].shape[0]
    place = lax.axis_index("expert")
    core = lax.axis_index("sys")
    factors = [
        [
            coefficient(table_ref, kind_ref, lax.rem(place + k, expert_size) * sys_size + core, place * experts + e)
            for e in range(experts)
        ]
        for k in range(expert_size)
    ]

    def step(block_ref, *parts):
        for start in range(0, tile, 16):
            span = pl.ds(start, 16)
            totals = [None] * expert_size
            for e in range(experts):
                weight = block_ref[e, span, :].astype(jnp.float32)
                for k in range(expert_size):
                    term = factors[k][e] * weight
                    totals[k] = term if totals[k] is None else totals[k] + term
            for k in range(expert_size):
                parts[k][span, :] = totals[k].astype(jnp.bfloat16)

    pltpu.emit_pipeline(
        step,
        grid=(rows // tile,),
        in_specs=[pl.BlockSpec((experts, tile, width), lambda i: (0, first // tile + i, 0))],
        out_specs=[pl.BlockSpec((tile, width), lambda i: (i, 0))] * expert_size,
    )(weights_ref, *out_refs)


def merge_part(table, kind, weights, expert_size, sys_size, first, rows, tile):
    experts, _, width = weights.shape
    return pl.pallas_call(
        functools.partial(merge_kernel, expert_size, sys_size, first, tile),
        in_specs=[
            pl.BlockSpec(memory_space=pltpu.SMEM),
            pl.BlockSpec(memory_space=pltpu.SMEM),
            pl.BlockSpec(memory_space=pltpu.HBM),
        ],
        out_specs=[pl.BlockSpec(memory_space=pl.ANY)] * expert_size,
        out_shape=[jax.ShapeDtypeStruct((rows, width), jnp.bfloat16)] * expert_size,
        compiler_params=pltpu.CompilerParams(vmem_limit_bytes=8 << 20),
        cost_estimate=pl.CostEstimate(
            flops=2 * expert_size * experts * rows * width,
            bytes_accessed=2 * experts * rows * width,
            transcendentals=0,
        ),
        name="merge",
    )(table, kind, weights)


def live_rows(grad_ref, counts_ref, sys_size):
    system = lax.axis_index("expert") * sys_size + lax.axis_index("sys")
    live = counts_ref[system] - lax.axis_index("edge") * grad_ref.shape[0]
    at = lax.broadcasted_iota(jnp.int32, grad_ref.shape, 0)
    return jnp.where(at < live, grad_ref[...], jnp.zeros((), grad_ref.dtype))


def outer_kernel(sys_size, counts_ref, features_ref, grad_ref, out_ref, masked):
    @pl.when(pl.program_id(0) == 0)
    def _():
        masked[...] = live_rows(grad_ref, counts_ref, sys_size)

    out_ref[...] = lax.dot_general(
        features_ref[...], masked[...], (((0,), (0,)), ((), ())), preferred_element_type=jnp.float32
    ).astype(out_ref.dtype)


def outer_products(counts, features, grad, sys_size, store_rows):
    edges, width_in = features.shape
    width = grad.shape[1]
    tile = 256 if width_in % 256 == 0 else width_in
    return pl.pallas_call(
        functools.partial(outer_kernel, sys_size),
        grid=(width_in // tile,),
        in_specs=[
            pl.BlockSpec(memory_space=pltpu.SMEM),
            pl.BlockSpec((edges, tile), lambda i: (0, i)),
            pl.BlockSpec((edges, width), lambda i: (0, 0)),
        ],
        out_specs=pl.BlockSpec((tile, width), lambda i: (i, 0)),
        out_shape=jax.ShapeDtypeStruct((store_rows, width), jnp.bfloat16),
        scratch_shapes=[pltpu.VMEM((edges, width), jnp.bfloat16)],
        compiler_params=pltpu.CompilerParams(vmem_limit_bytes=12 << 20),
        cost_estimate=pl.CostEstimate(
            flops=2 * edges * width_in * width,
            bytes_accessed=2 * (edges * width_in + edges * width + width_in * width),
            transcendentals=0,
        ),
        name="outer",
    )(counts, features, grad)


def input_kernel(sys_size, counts_ref, grad_ref, rows_ref, out_ref, masked):
    @pl.when(pl.program_id(0) == 0)
    def _():
        masked[...] = live_rows(grad_ref, counts_ref, sys_size)

    out_ref[...] = lax.dot_general(
        masked[...], rows_ref[...], (((1,), (1,)), ((), ())), preferred_element_type=jnp.float32
    ).astype(out_ref.dtype)


def input_product(counts, grad, store, sys_size, width_in):
    edges, width = grad.shape
    tile = 256 if width_in % 256 == 0 else width_in
    return pl.pallas_call(
        functools.partial(input_kernel, sys_size),
        grid=(width_in // tile,),
        in_specs=[
            pl.BlockSpec(memory_space=pltpu.SMEM),
            pl.BlockSpec((edges, width), lambda i: (0, 0)),
            pl.BlockSpec((tile, width), lambda i: (width_in // tile + i, 0)),
        ],
        out_specs=pl.BlockSpec((edges, tile), lambda i: (0, i)),
        out_shape=jax.ShapeDtypeStruct((edges, width_in), jnp.bfloat16),
        scratch_shapes=[pltpu.VMEM((edges, width), jnp.bfloat16)],
        compiler_params=pltpu.CompilerParams(vmem_limit_bytes=12 << 20),
        cost_estimate=pl.CostEstimate(
            flops=2 * edges * width_in * width,
            bytes_accessed=2 * (edges * width_in + edges * width + width_in * width),
            transcendentals=0,
        ),
        name="input_product",
    )(counts, grad, store)


def hop_kernel(count, take, add, send, rows, *refs):
    arrays, store, message = refs[1 : 1 + count], refs[1 + count], refs[2 + count :]
    if count:
        into = at_device(take) * rows
        adds = at_device(add) == 1
    if send is not None:
        origin = at_device(send) * rows

    if count:

        def update(i, _):
            span = pl.ds(pl.multiple_of(i * 16, 16), 16)
            here = pl.ds(pl.multiple_of(into + i * 16, 16), 16)
            total = arrays[0][span, :].astype(jnp.float32)
            for ref in arrays[1:]:
                total = total + ref[span, :].astype(jnp.float32)
            total = jnp.where(adds, store[here, :].astype(jnp.float32) + total, total)
            store[here, :] = total.astype(store.dtype)
            return 0

        lax.fori_loop(0, rows // 16, update, 0)
    if send is not None:

        def copy(i, _):
            span = pl.ds(pl.multiple_of(i * 16, 16), 16)
            message[0][span, :] = store[pl.ds(pl.multiple_of(origin + i * 16, 16), 16), :]
            return 0

        lax.fori_loop(0, rows // 16, copy, 0)


def hop(store, arrays, take, add, send, rows):
    width = store.shape[1]
    vmem = pl.BlockSpec(memory_space=pltpu.VMEM)
    shapes = [jax.ShapeDtypeStruct(store.shape, store.dtype)]
    if send is not None:
        shapes.append(jax.ShapeDtypeStruct((rows, width), store.dtype))
    return pl.pallas_call(
        functools.partial(hop_kernel, len(arrays), take, add, send, rows),
        in_specs=[vmem] * (1 + len(arrays)),
        out_specs=[vmem] * len(shapes),
        out_shape=shapes,
        input_output_aliases={0: 0},
        compiler_params=pltpu.CompilerParams(vmem_limit_bytes=1 << 20),
        cost_estimate=pl.CostEstimate(flops=rows * width, bytes_accessed=4 * rows * width, transcendentals=0),
        name="hop",
    )(store, *arrays)


def mix_kernel(expert_size, sys_size, scale, tile, table_ref, kind_ref, out_ref):
    width = out_ref.shape[1]
    slots = expert_size * sys_size
    experts = out_ref.shape[0] // tile
    place = lax.axis_index("expert")
    core = lax.axis_index("sys")
    line = lax.broadcasted_iota(jnp.int32, (tile, width), 0)
    lane = lax.broadcasted_iota(jnp.int32, (tile, width), 1)
    upper = lane < slots * tile
    lane = jnp.where(upper, lane, lane - slots * tile)
    slot_at = lane // tile
    hit = (lane - slot_at * tile) == line
    systems = [
        lax.rem(place + expert_size - k, expert_size) * sys_size + lax.rem(core + sys_size - l, sys_size)
        for l in range(sys_size)
        for k in range(expert_size)
    ]
    for e in range(experts):
        value = jnp.zeros((tile, width), jnp.float32)
        for slot, system in enumerate(systems):
            factor = coefficient(table_ref, kind_ref, system, place * experts + e) * scale
            value = jnp.where(slot_at == slot, factor, value)
        high = value.astype(jnp.bfloat16)
        low = (value - high.astype(jnp.float32)).astype(jnp.bfloat16)
        value = jnp.where(upper, high.astype(jnp.float32), low.astype(jnp.float32))
        out_ref[pl.ds(e * tile, tile), :] = jnp.where(hit, value, 0.0).astype(jnp.bfloat16)


def mix_matrix(table, kind, expert_size, sys_size, experts, scale, tile):
    width = 2 * expert_size * sys_size * tile
    return pl.pallas_call(
        functools.partial(mix_kernel, expert_size, sys_size, scale, tile),
        in_specs=[pl.BlockSpec(memory_space=pltpu.SMEM)] * 2,
        out_specs=pl.BlockSpec(memory_space=pltpu.VMEM),
        out_shape=jax.ShapeDtypeStruct((experts * tile, width), jnp.bfloat16),
        compiler_params=pltpu.CompilerParams(vmem_limit_bytes=4 << 20),
        cost_estimate=pl.CostEstimate(flops=10 * experts * tile * width, bytes_accessed=0, transcendentals=0),
        name="mix",
    )(table, kind)


def spread_kernel(count, groups, mix_ref, *refs):
    out_ref = refs[-1]
    experts, tile, width = out_ref.shape
    rows = jnp.concatenate([ref[...] for ref in refs[:count]], axis=0)
    rows = jnp.concatenate([rows, rows], axis=0)
    span = experts // groups
    for g in range(groups):
        part = jnp.dot(
            mix_ref[pl.ds(g * span * tile, span * tile), :], rows, preferred_element_type=jnp.float32
        )
        out_ref[pl.ds(g * span, span)] = part.astype(out_ref.dtype).reshape(span, tile, width)


def spread(mix, pieces, previous, experts, first, rows_all, tile):
    rows, width = pieces[0].shape
    count = len(pieces)
    groups = 4 if experts % 4 == 0 else 1
    specs = [pl.BlockSpec(mix.shape, lambda i: (0, 0))]
    specs += [pl.BlockSpec((tile, width), lambda i: (i, 0))] * count
    operands = [mix, *pieces]
    aliases = {}
    if previous is not None:
        specs.append(pl.BlockSpec(memory_space=pl.ANY))
        operands.append(previous)
        aliases = {len(operands) - 1: 0}
    return pl.pallas_call(
        functools.partial(spread_kernel, count, groups),
        grid=(rows // tile,),
        in_specs=specs,
        out_specs=pl.BlockSpec((experts, tile, width), lambda i: (0, first // tile + i, 0)),
        out_shape=jax.ShapeDtypeStruct((experts, rows_all, width), jnp.bfloat16),
        input_output_aliases=aliases,
        compiler_params=pltpu.CompilerParams(vmem_limit_bytes=16 << 20),
        cost_estimate=pl.CostEstimate(
            flops=2 * mix.size * rows // tile * width, bytes_accessed=2 * experts * rows * width, transcendentals=0
        ),
        name="spread",
    )(*operands)


def shift(size, by):
    return [(i, (i + by) % size) for i in range(size)]


def body(edge_inputs, out_grad, expert_weights, coef_table, system_kind, edge_counts):
    edge_size = lax.axis_size("edge")
    expert_size = lax.axis_size("expert")
    sys_size = lax.axis_size("sys")
    exp_local, row_count, width_out = expert_weights.shape
    width_in = edge_inputs.shape[2]
    edge_rows = out_grad.shape[1]
    chunks = 2 if row_count % 32 == 0 else 1
    rows = row_count // chunks
    tile = 32 if rows % 32 == 0 else 16
    features, grad = edge_inputs[0], out_grad[0]
    places = edge_size * chunks
    spare = 2 * places

    store = outer_products(edge_counts, features, grad, sys_size, (2 * places + 1) * rows)
    exchanged = []
    for h in range(chunks):
        parts = merge_part(
            coef_table, system_kind, expert_weights, expert_size, sys_size, h * rows, rows, tile
        )
        arrays = [parts[0]]
        arrays += [
            lax.ppermute(parts[k], "expert", shift(expert_size, k)) for k in range(1, expert_size)
        ]
        exchanged.append(arrays)

    scale = 1.0 / math.sqrt(edge_rows * edge_size)
    mix = mix_matrix(coef_table, system_kind, expert_size, sys_size, exp_local, scale, tile)

    steps = plan(edge_size, chunks, LAG, MERGED_AT)
    took = {}
    pending = []
    got = {}
    merged = set()
    waiting = {h: 2 * edge_size - 2 for h in range(chunks)}
    complete = {}

    def own(first):
        return [first + z * chunks for z in range(edge_size)]

    def settle(store, at, send):
        take, add = [spare] * edge_size, [0] * edge_size
        for source, target, kind, b, h in steps[at]:
            take[target] = b * chunks + h + (places if kind == "M" else 0)
            add[target] = int(kind == "S")
            if kind == "S" and b == target:
                waiting[h] -= 1
        return hop(store, [got.pop(at)], take, add, send, rows)

    def finish(store):
        for h in range(chunks):
            if waiting[h] == 0 and h not in complete:
                store, complete[h] = hop(store, [], None, None, own(h), rows)
        return store

    result = None
    for at, step in enumerate(steps):
        while pending and pending[0] < at - LAG:
            (store,) = settle(store, pending.pop(0), None)
            store = finish(store)
        for source, _, kind, b, h in step:
            if kind == "M" and b == source and h not in merged:
                merged.add(h)
                (store,) = hop(store, exchanged[h], own(places + h), [0] * edge_size, None, rows)
        if not step:
            continue
        send = [spare] * edge_size
        for source, _, kind, b, h in step:
            send[source] = b * chunks + h + (places if kind == "M" else 0)
        if pending and pending[0] <= at - LAG:
            store, message = settle(store, pending.pop(0), send)
        else:
            store, message = hop(store, [], None, None, send, rows)
        got[at] = lax.ppermute(message, "edge", [(source, target) for source, target, *_ in step])
        pending.append(at)
        store = finish(store)
    while pending:
        (store,) = settle(store, pending.pop(0), None)
        store = finish(store)

    for h in range(chunks):
        column = [complete[h]]
        for k in range(1, expert_size):
            column.append(lax.ppermute(complete[h], "expert", shift(expert_size, k)))
        pieces = list(column)
        for l in range(1, sys_size):
            pieces += [lax.ppermute(piece, "sys", shift(sys_size, l)) for piece in column]
        result = spread(mix, pieces, result, exp_local, h * rows, row_count, tile)

    input_grad = input_product(edge_counts, grad, store, sys_size, width_in)
    return (input_grad[None], result)


def solution(mesh):
    return jax.shard_map(
        body,
        mesh=mesh,
        in_specs=(
            P(("groups", "expert", "sys"), "edge", None),
            P(("groups", "expert", "sys"), "edge", None),
            P("expert", "edge", None),
            P(),
            P("groups"),
            P("groups"),
        ),
        out_specs=(
            P(("groups", "expert", "sys"), "edge", None),
            P(("groups", "expert"), "edge", None),
        ),
        check_vma=False,
    )
```

```python
import functools
import math

import jax
import jax.numpy as jnp
from jax import lax
from jax.experimental import pallas as pl
from jax.experimental.pallas import tpu as pltpu
from jax.sharding import PartitionSpec as P


LAG, EVEN_LAG, ODD_LAG = 3, 3, 3
MERGED_AT = (6, 8)
SPREAD_BEFORE = (15, 20)
MIX_BEFORE = 8
ENDS_GRANT = 62 << 20


def entry(values, at):
    return values[min(at, len(values) - 1)] + 4 * max(0, at - len(values) + 1)


def plan(size, chunks):
    sums = {}
    rows = {}
    for h in range(chunks):
        for b in range(size):
            rows[b, b, h] = (entry(MERGED_AT, h), entry(MERGED_AT, h), None)
            if b > 0:
                sums[0, 1, b, h] = (0, 0, None)
            if b < size - 1:
                sums[size - 1, -1, b, h] = (0, 0, None)
    sent = set()
    steps = []
    total = 2 * chunks * size * (size - 1)
    while len(sent) < total:
        at = len(steps)
        step = []
        for low in range(at % 2, size - 1, 2):
            for source, way in ((low, 1), (low + 1, -1)):
                target = source + way
                left = size - 1 - target if way == 1 else target
                ready = []
                for h in range(chunks):
                    for b in range(size):
                        ahead = (b - target) * way
                        for kind, state, order in (
                            ("S", sums.get((source, way, b, h)) if ahead >= 0 else None, (-ahead - 2, 0, h)),
                            ("M", rows.get((source, b, h)) if (source - b) * way >= 0 else None, (-left, 1, h)),
                        ):
                            if state and state[0] <= at and (kind, source, way, b, h) not in sent:
                                ready.append(((state[1] > at, *order), (kind, b, h), state[2]))
                if ready:
                    _, (kind, b, h), came = min(ready, key=lambda choice: choice[0])
                    sent.add((kind, source, way, b, h))
                    step.append((source, target, kind, b, h, came))
        lag = ODD_LAG if at % 2 else EVEN_LAG
        for source, target, kind, b, h, _ in step:
            if kind == "M":
                rows[target, b, h] = (at + lag, at + LAG, at)
            elif b != target:
                sums[target, target - source, b, h] = (at + lag, at + LAG, at)
        steps.append(step)
    return steps


def at_device(values):
    place = lax.axis_index("edge")
    result = jnp.int32(values[0])
    for z in range(1, len(values)):
        if values[z] != values[z - 1]:
            result = jnp.where(place >= z, jnp.int32(values[z]), result)
    return result


def coefficient(table_ref, kind_ref, system, expert):
    return table_ref[kind_ref[system], expert]


def merge_kernel(expert_size, sys_size, first, tile, table_ref, kind_ref, weights_ref, *out_refs):
    experts, _, width = weights_ref.shape
    rows = out_refs[0].shape[0]
    place = lax.axis_index("expert")
    core = lax.axis_index("sys")
    factors = [
        [
            coefficient(table_ref, kind_ref, lax.rem(place + k, expert_size) * sys_size + core, place * experts + e)
            for e in range(experts)
        ]
        for k in range(expert_size)
    ]

    def step(block_ref, *parts):
        for start in range(0, tile, 16):
            span = pl.ds(start, 16)
            totals = [None] * expert_size
            for e in range(experts):
                weight = block_ref[e, span, :].astype(jnp.float32)
                for k in range(expert_size):
                    term = factors[k][e] * weight
                    totals[k] = term if totals[k] is None else totals[k] + term
            for k in range(expert_size):
                parts[k][span, :] = totals[k].astype(jnp.bfloat16)

    pltpu.emit_pipeline(
        step,
        grid=(rows // tile,),
        in_specs=[pl.BlockSpec((experts, tile, width), lambda i: (0, first // tile + i, 0))],
        out_specs=[pl.BlockSpec((tile, width), lambda i: (i, 0))] * expert_size,
    )(weights_ref, *out_refs)


def merge_part(table, kind, weights, expert_size, sys_size, first, rows, tile):
    experts, _, width = weights.shape
    return pl.pallas_call(
        functools.partial(merge_kernel, expert_size, sys_size, first, tile),
        in_specs=[
            pl.BlockSpec(memory_space=pltpu.SMEM),
            pl.BlockSpec(memory_space=pltpu.SMEM),
            pl.BlockSpec(memory_space=pltpu.HBM),
        ],
        out_specs=[pl.BlockSpec(memory_space=pl.ANY)] * expert_size,
        out_shape=[jax.ShapeDtypeStruct((rows, width), jnp.bfloat16)] * expert_size,
        compiler_params=pltpu.CompilerParams(vmem_limit_bytes=8 << 20),
        cost_estimate=pl.CostEstimate(
            flops=2 * expert_size * experts * rows * width,
            bytes_accessed=2 * experts * rows * width,
            transcendentals=0,
        ),
        name="merge",
    )(table, kind, weights)


def live_rows(grad_ref, counts_ref, sys_size):
    system = lax.axis_index("expert") * sys_size + lax.axis_index("sys")
    live = counts_ref[system] - lax.axis_index("edge") * grad_ref.shape[0]
    at = lax.broadcasted_iota(jnp.int32, grad_ref.shape, 0)
    return jnp.where(at < live, grad_ref[...], jnp.zeros((), grad_ref.dtype))


def ends_kernel(sys_size, rows, starts, span, counts_ref, features_ref, grad_ref, *refs):
    outs, (features, grad, product, ready) = refs[:-4], refs[-4:]
    lanes = features.shape[1]
    first = at_device(starts)
    window = pl.multiple_of(at_device([one // 128 * 128 if one + lanes <= span else span - lanes for one in starts]), 128)
    loads = [
        pltpu.make_async_copy(grad_ref, grad, ready.at[0]),
        pltpu.make_async_copy(features_ref.at[:, pl.ds(window, lanes)], features, ready.at[1]),
    ]
    for load in loads:
        load.start()
    for load in loads:
        load.wait()
    product[...] = lax.dot_general(
        features[...],
        live_rows(grad, counts_ref, sys_size),
        (((0,), (0,)), ((), ())),
        preferred_element_type=jnp.float32,
    ).astype(product.dtype)
    for h, out_ref in enumerate(outs):
        out_ref[...] = product[pl.ds(pl.multiple_of(first - window + h * rows, 16), rows), :]


def end_products(counts, features, grad, sys_size, edge_size, chunks, rows):
    edges, width_in = features.shape
    width = grad.shape[1]
    block = chunks * rows
    starts = [0 if z else (edge_size - 1) * block for z in range(edge_size)]
    lanes = max(-(-(one % 128 + block) // 128) * 128 for one in starts)
    return pl.pallas_call(
        functools.partial(ends_kernel, sys_size, rows, starts, width_in),
        in_specs=[
            pl.BlockSpec(memory_space=pltpu.SMEM),
            pl.BlockSpec(memory_space=pl.ANY),
            pl.BlockSpec(memory_space=pl.ANY),
        ],
        out_specs=[pl.BlockSpec(memory_space=pltpu.VMEM)] * chunks,
        out_shape=[jax.ShapeDtypeStruct((rows, width), jnp.bfloat16)] * chunks,
        scratch_shapes=[
            pltpu.VMEM((edges, lanes), jnp.bfloat16),
            pltpu.VMEM((edges, width), jnp.bfloat16),
            pltpu.VMEM((lanes, width), jnp.bfloat16),
            pltpu.SemaphoreType.DMA((2,)),
        ],
        compiler_params=pltpu.CompilerParams(vmem_limit_bytes=ENDS_GRANT),
        cost_estimate=pl.CostEstimate(
            flops=2 * edges * lanes * width, bytes_accessed=2 * edges * (lanes + width), transcendentals=0
        ),
        name="ends",
    )(counts, features, grad)


def outer_kernel(sys_size, counts_ref, features_ref, grad_ref, out_ref, masked):
    @pl.when(pl.program_id(0) == 0)
    def _():
        masked[...] = live_rows(grad_ref, counts_ref, sys_size)

    out_ref[...] = lax.dot_general(
        features_ref[...], masked[...], (((0,), (0,)), ((), ())), preferred_element_type=jnp.float32
    ).astype(out_ref.dtype)


def outer_products(counts, features, grad, sys_size, store_rows):
    edges, width_in = features.shape
    width = grad.shape[1]
    tile = 256 if width_in % 256 == 0 else width_in
    return pl.pallas_call(
        functools.partial(outer_kernel, sys_size),
        grid=(width_in // tile,),
        in_specs=[
            pl.BlockSpec(memory_space=pltpu.SMEM),
            pl.BlockSpec((edges, tile), lambda i: (0, i)),
            pl.BlockSpec((edges, width), lambda i: (0, 0)),
        ],
        out_specs=pl.BlockSpec((tile, width), lambda i: (i, 0)),
        out_shape=jax.ShapeDtypeStruct((store_rows, width), jnp.bfloat16),
        scratch_shapes=[pltpu.VMEM((edges, width), jnp.bfloat16)],
        compiler_params=pltpu.CompilerParams(vmem_limit_bytes=12 << 20),
        cost_estimate=pl.CostEstimate(
            flops=2 * edges * width_in * width,
            bytes_accessed=2 * (edges * width_in + edges * width + width_in * width),
            transcendentals=0,
        ),
        name="outer",
    )(counts, features, grad)


def input_kernel(sys_size, counts_ref, grad_ref, rows_ref, out_ref, live_ref):
    @pl.when(pl.program_id(0) == 0)
    def _():
        live_ref[...] = live_rows(grad_ref, counts_ref, sys_size)

    out_ref[...] = lax.dot_general(
        live_ref[...], rows_ref[...], (((1,), (1,)), ((), ())), preferred_element_type=jnp.float32
    ).astype(out_ref.dtype)


def input_product(counts, grad, store, sys_size, width_in):
    edges, width = grad.shape
    tile = 256 if width_in % 256 == 0 else width_in
    return pl.pallas_call(
        functools.partial(input_kernel, sys_size),
        grid=(width_in // tile,),
        in_specs=[
            pl.BlockSpec(memory_space=pltpu.SMEM),
            pl.BlockSpec((edges, width), lambda i: (0, 0)),
            pl.BlockSpec((tile, width), lambda i: (width_in // tile + i, 0)),
        ],
        out_specs=[
            pl.BlockSpec((edges, tile), lambda i: (0, i)),
            pl.BlockSpec((edges, width), lambda i: (0, 0)),
        ],
        out_shape=[
            jax.ShapeDtypeStruct((edges, width_in), jnp.bfloat16),
            jax.ShapeDtypeStruct((edges, width), jnp.bfloat16),
        ],
        compiler_params=pltpu.CompilerParams(vmem_limit_bytes=12 << 20),
        cost_estimate=pl.CostEstimate(
            flops=2 * edges * width_in * width,
            bytes_accessed=2 * (edges * width_in + edges * width + width_in * width),
            transcendentals=0,
        ),
        name="input_product",
    )(counts, grad, store)


def last_kernel(width_in, windows, live_ref, store_ref, _, out_ref, part, done):
    lanes = part.shape[1]
    first = pl.multiple_of(at_device(windows), 128)
    part[...] = lax.dot_general(
        live_ref[...],
        store_ref[pl.ds(pl.multiple_of(width_in + first, 128), lanes), :],
        (((1,), (1,)), ((), ())),
        preferred_element_type=jnp.float32,
    ).astype(part.dtype)
    write = pltpu.make_async_copy(part, out_ref.at[:, pl.ds(first, lanes)], done)
    write.start()
    write.wait()


def last_product(live, store, product, rows, places):
    edges, width_in = product.shape
    lanes = min(width_in, max(-(-(place * rows % 128 + rows) // 128) * 128 for place in places))
    windows = [min(place * rows // 128 * 128, width_in - lanes) for place in places]
    vmem = pl.BlockSpec(memory_space=pltpu.VMEM)
    return pl.pallas_call(
        functools.partial(last_kernel, width_in, windows),
        in_specs=[vmem, vmem, pl.BlockSpec(memory_space=pl.ANY)],
        out_specs=pl.BlockSpec(memory_space=pl.ANY),
        out_shape=jax.ShapeDtypeStruct(product.shape, product.dtype),
        input_output_aliases={2: 0},
        scratch_shapes=[pltpu.VMEM((edges, lanes), jnp.bfloat16), pltpu.SemaphoreType.DMA],
        compiler_params=pltpu.CompilerParams(vmem_limit_bytes=4 << 20),
        cost_estimate=pl.CostEstimate(
            flops=2 * edges * lanes * live.shape[1], bytes_accessed=2 * edges * lanes, transcendentals=0
        ),
        name="last_product",
    )(live, store, product)


def hop_kernel(count, behind, take, add, send, rows, *refs):
    arrays, (store, *message) = refs[1 : 1 + count], refs[1 + count + behind :]
    if count:
        into = at_device(take) * rows
        adds = at_device(add) == 1
    if send is not None:
        origin = at_device(send) * rows

    if count:

        def update(i, _):
            span = pl.ds(pl.multiple_of(i * 16, 16), 16)
            here = pl.ds(pl.multiple_of(into + i * 16, 16), 16)
            total = arrays[0][span, :].astype(jnp.float32)
            for ref in arrays[1:]:
                total = total + ref[span, :].astype(jnp.float32)
            total = jnp.where(adds, store[here, :].astype(jnp.float32) + total, total)
            store[here, :] = total.astype(store.dtype)
            return 0

        lax.fori_loop(0, rows // 16, update, 0)
    if send is not None:

        def copy(i, _):
            span = pl.ds(pl.multiple_of(i * 16, 16), 16)
            message[0][span, :] = store[pl.ds(pl.multiple_of(origin + i * 16, 16), 16), :]
            return 0

        lax.fori_loop(0, rows // 16, copy, 0)


def hop(store, arrays, take, add, send, rows, behind=()):
    width = store.shape[1]
    vmem = pl.BlockSpec(memory_space=pltpu.VMEM)
    shapes = [jax.ShapeDtypeStruct(store.shape, store.dtype)]
    if send is not None:
        shapes.append(jax.ShapeDtypeStruct((rows, width), store.dtype))
    return pl.pallas_call(
        functools.partial(hop_kernel, len(arrays), len(behind), take, add, send, rows),
        in_specs=[vmem] * (1 + len(arrays)) + [pl.BlockSpec(memory_space=pl.ANY)] * len(behind),
        out_specs=[vmem] * len(shapes),
        out_shape=shapes,
        input_output_aliases={0: 0},
        compiler_params=pltpu.CompilerParams(vmem_limit_bytes=1 << 20),
        cost_estimate=pl.CostEstimate(flops=rows * width, bytes_accessed=4 * rows * width, transcendentals=0),
        name="hop",
    )(store, *arrays, *behind)


def mix_kernel(expert_size, sys_size, scale, tile, table_ref, kind_ref, out_ref):
    width = out_ref.shape[1]
    slots = expert_size * sys_size
    experts = out_ref.shape[0] // tile
    place = lax.axis_index("expert")
    core = lax.axis_index("sys")
    line = lax.broadcasted_iota(jnp.int32, (tile, width), 0)
    lane = lax.broadcasted_iota(jnp.int32, (tile, width), 1)
    upper = lane < slots * tile
    lane = jnp.where(upper, lane, lane - slots * tile)
    slot_at = lane // tile
    hit = (lane - slot_at * tile) == line
    systems = [
        lax.rem(place + expert_size - k, expert_size) * sys_size + lax.rem(core + sys_size - l, sys_size)
        for l in range(sys_size)
        for k in range(expert_size)
    ]
    for e in range(experts):
        value = jnp.zeros((tile, width), jnp.float32)
        for slot, system in enumerate(systems):
            factor = coefficient(table_ref, kind_ref, system, place * experts + e) * scale
            value = jnp.where(slot_at == slot, factor, value)
        high = value.astype(jnp.bfloat16)
        low = (value - high.astype(jnp.float32)).astype(jnp.bfloat16)
        value = jnp.where(upper, high.astype(jnp.float32), low.astype(jnp.float32))
        out_ref[pl.ds(e * tile, tile), :] = jnp.where(hit, value, 0.0).astype(jnp.bfloat16)


def mix_matrix(table, kind, expert_size, sys_size, experts, scale, tile):
    width = 2 * expert_size * sys_size * tile
    return pl.pallas_call(
        functools.partial(mix_kernel, expert_size, sys_size, scale, tile),
        in_specs=[pl.BlockSpec(memory_space=pltpu.SMEM)] * 2,
        out_specs=pl.BlockSpec(memory_space=pltpu.VMEM),
        out_shape=jax.ShapeDtypeStruct((experts * tile, width), jnp.bfloat16),
        compiler_params=pltpu.CompilerParams(vmem_limit_bytes=4 << 20),
        cost_estimate=pl.CostEstimate(flops=10 * experts * tile * width, bytes_accessed=0, transcendentals=0),
        name="mix",
    )(table, kind)


def spread_kernel(count, groups, mix_ref, *refs):
    out_ref, token_ref = refs[-2:]
    token_ref[...] = jnp.zeros_like(token_ref)
    experts, tile, width = out_ref.shape
    rows = jnp.concatenate([ref[...] for ref in refs[:count]], axis=0)
    rows = jnp.concatenate([rows, rows], axis=0)
    span = experts // groups
    for g in range(groups):
        part = jnp.dot(
            mix_ref[pl.ds(g * span * tile, span * tile), :], rows, preferred_element_type=jnp.float32
        )
        out_ref[pl.ds(g * span, span)] = part.astype(out_ref.dtype).reshape(span, tile, width)


def spread(mix, pieces, previous, experts, first, rows_all, tile):
    rows, width = pieces[0].shape
    count = len(pieces)
    groups = 4 if experts % 4 == 0 else 1
    specs = [pl.BlockSpec(mix.shape, lambda i: (0, 0))]
    specs += [pl.BlockSpec((tile, width), lambda i: (i, 0))] * count
    operands = [mix, *pieces]
    aliases = {}
    if previous is not None:
        specs.append(pl.BlockSpec(memory_space=pl.ANY))
        operands.append(previous)
        aliases = {len(operands) - 1: 0}
    return pl.pallas_call(
        functools.partial(spread_kernel, count, groups),
        grid=(rows // tile,),
        in_specs=specs,
        out_specs=[
            pl.BlockSpec((experts, tile, width), lambda i: (0, first // tile + i, 0)),
            pl.BlockSpec((8, 128), lambda i: (0, 0)),
        ],
        out_shape=[
            jax.ShapeDtypeStruct((experts, rows_all, width), jnp.bfloat16),
            jax.ShapeDtypeStruct((8, 128), jnp.float32),
        ],
        input_output_aliases=aliases,
        compiler_params=pltpu.CompilerParams(vmem_limit_bytes=16 << 20),
        cost_estimate=pl.CostEstimate(
            flops=2 * mix.size * rows // tile * width, bytes_accessed=2 * experts * rows * width, transcendentals=0
        ),
        name="spread",
    )(*operands)


def swaps(at, edge_size, sys_size):
    pairs = []
    for z in range(edge_size):
        other = z + 1 if (z - at) % 2 == 0 else z - 1
        for core in range(sys_size):
            if 0 <= other < edge_size:
                pairs.append((z * sys_size + core, other * sys_size + core))
            elif sys_size % 2 == 0:
                pairs.append((z * sys_size + core, z * sys_size + (core ^ 1)))
    return pairs


def shift(size, by):
    return [(i, (i + by) % size) for i in range(size)]


def chunks_of(row_count):
    return 2 if row_count % 32 == 0 else 1


def body(edge_inputs, out_grad, expert_weights, coef_table, system_kind, edge_counts):
    edge_size = lax.axis_size("edge")
    expert_size = lax.axis_size("expert")
    sys_size = lax.axis_size("sys")
    exp_local, row_count, _ = expert_weights.shape
    width_in = edge_inputs.shape[2]
    edge_rows = out_grad.shape[1]
    chunks = chunks_of(row_count)
    rows = row_count // chunks
    tile = 32 if rows % 32 == 0 else 16
    features, grad = edge_inputs[0], out_grad[0]
    places = edge_size * chunks
    spare = 2 * places

    scale = 1.0 / math.sqrt(edge_rows * edge_size)
    mix = mix_matrix(coef_table, system_kind, expert_size, sys_size, exp_local, scale, tile)

    firsts = end_products(edge_counts, features, grad, sys_size, edge_size, chunks, rows)
    store = outer_products(edge_counts, features, grad, sys_size, (2 * places + 1) * rows)
    exchanged = []
    for h in range(chunks):
        parts = merge_part(
            coef_table, system_kind, expert_weights, expert_size, sys_size, h * rows, rows, tile
        )
        arrays = [parts[0]]
        arrays += [lax.ppermute(parts[k], "expert", shift(expert_size, k)) for k in range(1, expert_size)]
        exchanged.append(arrays)

    steps = plan(edge_size, chunks)
    pending = []
    got = {}
    merged = set()
    waiting = {h: 2 * edge_size - 2 for h in range(chunks)}
    taken = set()
    result = None

    def own(first):
        return [first + z * chunks for z in range(edge_size)]

    def settle(store, at, origin, behind=()):
        take, add = [spare] * edge_size, [0] * edge_size
        for _, target, kind, b, h, _ in steps[at]:
            take[target] = b * chunks + h + (places if kind == "M" else 0)
            add[target] = int(kind == "S")
            if kind == "S" and b == target:
                waiting[h] -= 1
        pending.remove(at)
        return hop(store, [got.pop(at)], take, add, origin, rows, behind)

    tokens = {}
    mixed = [mix]

    def overdue(at):
        late = [tokens.pop(h) for h in list(tokens) if at >= entry(SPREAD_BEFORE, h)]
        if mixed and at >= MIX_BEFORE:
            late.append(mixed.pop())
        return late

    def finish(store, result):
        for h in range(chunks):
            if waiting[h] or h in taken:
                continue
            taken.add(h)
            store, rows_h = hop(store, [], None, None, own(h), rows)
            column = [rows_h]
            for k in range(1, expert_size):
                column.append(lax.ppermute(rows_h, "expert", shift(expert_size, k)))
            pieces = list(column)
            for l in range(1, sys_size):
                pieces += [lax.ppermute(piece, "sys", shift(sys_size, l)) for piece in column]
            result, token = spread(mix, pieces, result, exp_local, h * rows, row_count, tile)
            tokens[h] = token
        return store, result

    for at, step in enumerate(steps):
        if not step:
            continue
        for source, _, kind, b, h, _ in step:
            if kind == "M" and b == source and h not in merged:
                merged.add(h)
                (store,) = hop(store, exchanged[h], own(places + h), [0] * edge_size, None, rows)
        origin = [spare] * edge_size
        for source, _, kind, b, h, _ in step:
            origin[source] = b * chunks + h + (places if kind == "M" else 0)
        needed = {came for *_, came in step}
        due = [one for one in pending if one in needed or one <= at - LAG]
        for one in due[:-1]:
            (store,) = settle(store, one, None)
        if all((kind, b) == ("S", 0 if source else edge_size - 1) and came is None for source, _, kind, b, _, came in step):
            message = firsts[step[0][4]]
        elif due:
            store, message = settle(store, due[-1], origin, overdue(at))
        else:
            store, message = hop(store, [], None, None, origin, rows, overdue(at))
        got[at] = lax.ppermute(message, ("edge", "sys"), swaps(at, edge_size, sys_size))
        pending.append(at)
        store, result = finish(store, result)
    while len(pending) > 1:
        (store,) = settle(store, pending[0], None, list(tokens.values()) if len(pending) == 2 else ())
        store, result = finish(store, result)
    product, live = input_product(edge_counts, grad, store, sys_size, width_in)
    last = [0] * edge_size
    for _, target, _, b, h, _ in steps[pending[0]]:
        last[target] = b * chunks + h
    (store,) = settle(store, pending[0], None, (live,))
    store, result = finish(store, result)
    input_grad = last_product(live, store, product, rows, last)
    return (input_grad[None], result)


def solution(mesh):
    specs = dict(
        mesh=mesh,
        in_specs=(
            P(("groups", "expert", "sys"), "edge", None),
            P(("groups", "expert", "sys"), "edge", None),
            P("expert", "edge", None),
            P(),
            P("groups"),
            P("groups"),
        ),
        out_specs=(
            P(("groups", "expert", "sys"), "edge", None),
            P(("groups", "expert"), "edge", None),
        ),
        check_vma=False,
    )

    def program(*args):
        return jax.shard_map(body, **specs)(*args)

    return program
```

```python
import functools
import math

import jax
import jax.numpy as jnp
from jax import lax
from jax.experimental import pallas as pl
from jax.experimental.pallas import tpu as pltpu
from jax.sharding import PartitionSpec as P


LAG = 3
SPLIT = ()
SKIPPED = (4,)
SUMS_FIRST, SUMS_CHUNK, ROWS_CHUNK, OWN_WEIGHT = 3, 1, 0, -0.7
MERGED_AT = (6, 8)
SPREAD_BEFORE = (17, 99)
MIX_BEFORE = 12
ENDS_GRANT = 62 << 20
MERGES_TOGETHER = True


def entry(values, at):
    return values[min(at, len(values) - 1)] + 4 * max(0, at - len(values) + 1)


def plan(size, chunks, halves):
    sums = {}
    rows = {}
    for h in range(chunks):
        for b in range(size):
            rows[b, b, h] = (entry(MERGED_AT, h), entry(MERGED_AT, h), None)
            if b > 0:
                sums[0, 1, b, h] = (0, 0, None)
            if b < size - 1:
                sums[size - 1, -1, b, h] = (0, 0, None)
    sent = set()
    steps = []
    total = 2 * chunks * size * (size - 1)
    while len(sent) < total:
        at = len(steps)
        step = []
        for low in range(at % 2, 0 if at in SKIPPED else size - 1, 2):
            for source, way in ((low, 1), (low + 1, -1)):
                target = source + way
                left = size - 1 - target if way == 1 else target
                ready = []
                for h in range(chunks):
                    for b in range(size):
                        ahead = (b - target) * way
                        own = OWN_WEIGHT if b == source else 0
                        for kind, state, order in (
                            ("S", sums.get((source, way, b, h)) if ahead >= 0 else None, SUMS_CHUNK * h - ahead - SUMS_FIRST),
                            ("M", rows.get((source, b, h)) if (source - b) * way >= 0 else None, ROWS_CHUNK * h - left + own),
                        ):
                            if state and state[0] <= at and (kind, source, way, b, h) not in sent:
                                ready.append(((state[1] > at, order, kind != "S", h), (kind, b, h), state[2]))
                if ready:
                    _, (kind, b, h), came = min(ready, key=lambda choice: choice[0])
                    sent.add((kind, source, way, b, h))
                    step.append((source, target, kind, b, h, came))
        lag = 1 if halves and at % 2 and at in SPLIT else LAG
        for source, target, kind, b, h, _ in step:
            if kind == "M":
                rows[target, b, h] = (at + lag, at + LAG, at)
            elif b != target:
                sums[target, target - source, b, h] = (at + lag, at + LAG, at)
        steps.append(step)
    return steps


def parts_of(at, halves):
    return (0, 1) if halves and at in SPLIT else (None,)


def layout(row_count):
    chunks = 2 if row_count % 32 == 0 else 1
    rows = row_count // chunks
    return chunks, rows, rows % 32 == 0


def at_device(values):
    place = lax.axis_index("edge")
    result = jnp.int32(values[0])
    for z in range(1, len(values)):
        if values[z] != values[z - 1]:
            result = jnp.where(place >= z, jnp.int32(values[z]), result)
    return result


def coefficient(table_ref, kind_ref, system, expert):
    return table_ref[kind_ref[system], expert]


def merge_kernel(expert_size, sys_size, first, tile, table_ref, kind_ref, weights_ref, *out_refs):
    experts, _, width = weights_ref.shape
    rows = out_refs[0].shape[0]
    place = lax.axis_index("expert")
    core = lax.axis_index("sys")
    factors = [
        [
            coefficient(table_ref, kind_ref, lax.rem(place + k, expert_size) * sys_size + core, place * experts + e)
            for e in range(experts)
        ]
        for k in range(expert_size)
    ]

    def step(block_ref, *parts):
        for start in range(0, tile, 16):
            span = pl.ds(start, 16)
            totals = [None] * expert_size
            for e in range(experts):
                weight = block_ref[e, span, :].astype(jnp.float32)
                for k in range(expert_size):
                    term = factors[k][e] * weight
                    totals[k] = term if totals[k] is None else totals[k] + term
            for k in range(expert_size):
                parts[k][span, :] = totals[k].astype(jnp.bfloat16)

    pltpu.emit_pipeline(
        step,
        grid=(rows // tile,),
        in_specs=[pl.BlockSpec((experts, tile, width), lambda i: (0, first // tile + i, 0))],
        out_specs=[pl.BlockSpec((tile, width), lambda i: (i, 0))] * expert_size,
    )(weights_ref, *out_refs)


def merge_part(table, kind, weights, expert_size, sys_size, first, rows, tile):
    experts, _, width = weights.shape
    return pl.pallas_call(
        functools.partial(merge_kernel, expert_size, sys_size, first, tile),
        in_specs=[
            pl.BlockSpec(memory_space=pltpu.SMEM),
            pl.BlockSpec(memory_space=pltpu.SMEM),
            pl.BlockSpec(memory_space=pltpu.HBM),
        ],
        out_specs=[pl.BlockSpec(memory_space=pl.ANY)] * expert_size,
        out_shape=[jax.ShapeDtypeStruct((rows, width), jnp.bfloat16)] * expert_size,
        compiler_params=pltpu.CompilerParams(vmem_limit_bytes=8 << 20),
        cost_estimate=pl.CostEstimate(
            flops=2 * expert_size * experts * rows * width,
            bytes_accessed=2 * experts * rows * width,
            transcendentals=0,
        ),
        name="merge",
    )(table, kind, weights)


def live_rows(grad_ref, counts_ref, sys_size):
    system = lax.axis_index("expert") * sys_size + lax.axis_index("sys")
    live = counts_ref[system] - lax.axis_index("edge") * grad_ref.shape[0]
    at = lax.broadcasted_iota(jnp.int32, grad_ref.shape, 0)
    return jnp.where(at < live, grad_ref[...], jnp.zeros((), grad_ref.dtype))


def ends_kernel(sys_size, pieces, starts, span, counts_ref, features_ref, grad_ref, *refs):
    outs, (features, grad, product, ready) = refs[:-4], refs[-4:]
    lanes = features.shape[1]
    first = at_device(starts)
    window = pl.multiple_of(at_device([one // 128 * 128 if one + lanes <= span else span - lanes for one in starts]), 128)
    loads = [
        pltpu.make_async_copy(grad_ref, grad, ready.at[0]),
        pltpu.make_async_copy(features_ref.at[:, pl.ds(window, lanes)], features, ready.at[1]),
    ]
    for load in loads:
        load.start()
    for load in loads:
        load.wait()
    product[...] = lax.dot_general(
        features[...],
        live_rows(grad, counts_ref, sys_size),
        (((0,), (0,)), ((), ())),
        preferred_element_type=jnp.float32,
    ).astype(product.dtype)
    for (start, rows), out_ref in zip(pieces, outs):
        out_ref[...] = product[pl.ds(pl.multiple_of(first - window + start, 16), rows), :]


def end_products(counts, features, grad, sys_size, edge_size, block, pieces):
    edges, width_in = features.shape
    width = grad.shape[1]
    base = min(start for start, _ in pieces)
    extent = max(start + rows for start, rows in pieces) - base
    starts = [base + (0 if z else (edge_size - 1) * block) for z in range(edge_size)]
    lanes = min(width_in, max(-(-(one % 128 + extent) // 128) * 128 for one in starts))
    pieces = [(start - base, rows) for start, rows in pieces]
    return pl.pallas_call(
        functools.partial(ends_kernel, sys_size, pieces, starts, width_in),
        in_specs=[
            pl.BlockSpec(memory_space=pltpu.SMEM),
            pl.BlockSpec(memory_space=pl.ANY),
            pl.BlockSpec(memory_space=pl.ANY),
        ],
        out_specs=[pl.BlockSpec(memory_space=pltpu.VMEM)] * len(pieces),
        out_shape=[jax.ShapeDtypeStruct((rows, width), jnp.bfloat16) for _, rows in pieces],
        scratch_shapes=[
            pltpu.VMEM((edges, lanes), jnp.bfloat16),
            pltpu.VMEM((edges, width), jnp.bfloat16),
            pltpu.VMEM((lanes, width), jnp.bfloat16),
            pltpu.SemaphoreType.DMA((2,)),
        ],
        compiler_params=pltpu.CompilerParams(vmem_limit_bytes=ENDS_GRANT),
        cost_estimate=pl.CostEstimate(
            flops=2 * edges * lanes * width, bytes_accessed=2 * edges * (lanes + width), transcendentals=0
        ),
        name="ends",
    )(counts, features, grad)


def outer_kernel(sys_size, counts_ref, features_ref, grad_ref, out_ref, live_ref):
    @pl.when(pl.program_id(0) == 0)
    def _():
        live_ref[...] = live_rows(grad_ref, counts_ref, sys_size)

    out_ref[...] = lax.dot_general(
        features_ref[...], live_ref[...], (((0,), (0,)), ((), ())), preferred_element_type=jnp.float32
    ).astype(out_ref.dtype)


def outer_products(counts, features, grad, sys_size, store_rows):
    edges, width_in = features.shape
    width = grad.shape[1]
    tile = 256 if width_in % 256 == 0 else width_in
    return pl.pallas_call(
        functools.partial(outer_kernel, sys_size),
        grid=(width_in // tile,),
        in_specs=[
            pl.BlockSpec(memory_space=pltpu.SMEM),
            pl.BlockSpec((edges, tile), lambda i: (0, i)),
            pl.BlockSpec((edges, width), lambda i: (0, 0)),
        ],
        out_specs=[
            pl.BlockSpec((tile, width), lambda i: (i, 0)),
            pl.BlockSpec((edges, width), lambda i: (0, 0)),
        ],
        out_shape=[
            jax.ShapeDtypeStruct((store_rows, width), jnp.bfloat16),
            jax.ShapeDtypeStruct((edges, width), jnp.bfloat16),
        ],
        compiler_params=pltpu.CompilerParams(vmem_limit_bytes=12 << 20),
        cost_estimate=pl.CostEstimate(
            flops=2 * edges * width_in * width,
            bytes_accessed=2 * (edges * width_in + edges * width + width_in * width),
            transcendentals=0,
        ),
        name="outer",
    )(counts, features, grad)


def input_kernel(live_ref, rows_ref, out_ref):
    out_ref[...] = lax.dot_general(
        live_ref[...], rows_ref[...], (((1,), (1,)), ((), ())), preferred_element_type=jnp.float32
    ).astype(out_ref.dtype)


def input_product(live, store, width_in):
    edges, width = live.shape
    tile = 256 if width_in % 256 == 0 else width_in
    return pl.pallas_call(
        input_kernel,
        grid=(width_in // tile,),
        in_specs=[
            pl.BlockSpec((edges, width), lambda i: (0, 0)),
            pl.BlockSpec((tile, width), lambda i: (width_in // tile + i, 0)),
        ],
        out_specs=pl.BlockSpec((edges, tile), lambda i: (0, i)),
        out_shape=jax.ShapeDtypeStruct((edges, width_in), jnp.bfloat16),
        compiler_params=pltpu.CompilerParams(vmem_limit_bytes=12 << 20),
        cost_estimate=pl.CostEstimate(
            flops=2 * edges * width_in * width,
            bytes_accessed=2 * (edges * width_in + edges * width + width_in * width),
            transcendentals=0,
        ),
        name="input_product",
    )(live, store)


def last_kernel(width_in, windows, live_ref, store_ref, _, out_ref, part, done):
    lanes = part.shape[1]
    first = pl.multiple_of(at_device(windows), 128)
    part[...] = lax.dot_general(
        live_ref[...],
        store_ref[pl.ds(pl.multiple_of(width_in + first, 128), lanes), :],
        (((1,), (1,)), ((), ())),
        preferred_element_type=jnp.float32,
    ).astype(part.dtype)
    write = pltpu.make_async_copy(part, out_ref.at[:, pl.ds(first, lanes)], done)
    write.start()
    write.wait()


def last_product(live, store, product, rows, places):
    edges, width_in = product.shape
    lanes = min(width_in, max(-(-(place * rows % 128 + rows) // 128) * 128 for place in places))
    windows = [min(place * rows // 128 * 128, width_in - lanes) for place in places]
    vmem = pl.BlockSpec(memory_space=pltpu.VMEM)
    return pl.pallas_call(
        functools.partial(last_kernel, width_in, windows),
        in_specs=[vmem, vmem, pl.BlockSpec(memory_space=pl.ANY)],
        out_specs=pl.BlockSpec(memory_space=pl.ANY),
        out_shape=jax.ShapeDtypeStruct(product.shape, product.dtype),
        input_output_aliases={2: 0},
        scratch_shapes=[pltpu.VMEM((edges, lanes), jnp.bfloat16), pltpu.SemaphoreType.DMA],
        compiler_params=pltpu.CompilerParams(vmem_limit_bytes=4 << 20),
        cost_estimate=pl.CostEstimate(
            flops=2 * edges * lanes * live.shape[1], bytes_accessed=2 * edges * lanes, transcendentals=0
        ),
        name="last_product",
    )(live, store, product)


def hop_kernel(count, behind, take, add, origin, *refs):
    arrays, (store, *message) = refs[1 : 1 + count], refs[1 + count + behind :]
    if count:
        into = at_device(take)
        adds = at_device(add) == 1

        def update(i, _):
            span = pl.ds(pl.multiple_of(i * 16, 16), 16)
            here = pl.ds(pl.multiple_of(into + i * 16, 16), 16)
            total = arrays[0][span, :].astype(jnp.float32)
            for ref in arrays[1:]:
                total = total + ref[span, :].astype(jnp.float32)
            total = jnp.where(adds, store[here, :].astype(jnp.float32) + total, total)
            store[here, :] = total.astype(store.dtype)
            return 0

        lax.fori_loop(0, arrays[0].shape[0] // 16, update, 0)
    if message:
        out = message[0]
        first = at_device(origin)

        def copy(i, _):
            span = pl.ds(pl.multiple_of(i * 16, 16), 16)
            out[span, :] = store[pl.ds(pl.multiple_of(first + i * 16, 16), 16), :]
            return 0

        lax.fori_loop(0, out.shape[0] // 16, copy, 0)


def hop(store, arrays, take, add, origin, rows, behind=()):
    width = store.shape[1]
    vmem = pl.BlockSpec(memory_space=pltpu.VMEM)
    shapes = [jax.ShapeDtypeStruct(store.shape, store.dtype)]
    if origin is not None:
        shapes.append(jax.ShapeDtypeStruct((rows, width), store.dtype))
    return pl.pallas_call(
        functools.partial(hop_kernel, len(arrays), len(behind), take, add, origin),
        in_specs=[vmem] * (1 + len(arrays)) + [pl.BlockSpec(memory_space=pl.ANY)] * len(behind),
        out_specs=[vmem] * len(shapes),
        out_shape=shapes,
        input_output_aliases={0: 0},
        compiler_params=pltpu.CompilerParams(vmem_limit_bytes=1 << 20),
        cost_estimate=pl.CostEstimate(flops=rows * width, bytes_accessed=4 * rows * width, transcendentals=0),
        name="hop",
    )(store, *arrays, *behind)


def mix_kernel(expert_size, sys_size, scale, tile, table_ref, kind_ref, out_ref):
    width = out_ref.shape[1]
    slots = expert_size * sys_size
    experts = out_ref.shape[0] // tile
    place = lax.axis_index("expert")
    core = lax.axis_index("sys")
    line = lax.broadcasted_iota(jnp.int32, (tile, width), 0)
    lane = lax.broadcasted_iota(jnp.int32, (tile, width), 1)
    upper = lane < slots * tile
    lane = jnp.where(upper, lane, lane - slots * tile)
    slot_at = lane // tile
    hit = (lane - slot_at * tile) == line
    systems = [
        lax.rem(place + expert_size - k, expert_size) * sys_size + lax.rem(core + sys_size - l, sys_size)
        for l in range(sys_size)
        for k in range(expert_size)
    ]
    for e in range(experts):
        value = jnp.zeros((tile, width), jnp.float32)
        for slot, system in enumerate(systems):
            factor = coefficient(table_ref, kind_ref, system, place * experts + e) * scale
            value = jnp.where(slot_at == slot, factor, value)
        high = value.astype(jnp.bfloat16)
        low = (value - high.astype(jnp.float32)).astype(jnp.bfloat16)
        value = jnp.where(upper, high.astype(jnp.float32), low.astype(jnp.float32))
        out_ref[pl.ds(e * tile, tile), :] = jnp.where(hit, value, 0.0).astype(jnp.bfloat16)


def mix_matrix(table, kind, expert_size, sys_size, experts, scale, tile):
    width = 2 * expert_size * sys_size * tile
    return pl.pallas_call(
        functools.partial(mix_kernel, expert_size, sys_size, scale, tile),
        in_specs=[pl.BlockSpec(memory_space=pltpu.SMEM)] * 2,
        out_specs=pl.BlockSpec(memory_space=pltpu.VMEM),
        out_shape=jax.ShapeDtypeStruct((experts * tile, width), jnp.bfloat16),
        compiler_params=pltpu.CompilerParams(vmem_limit_bytes=4 << 20),
        cost_estimate=pl.CostEstimate(flops=10 * experts * tile * width, bytes_accessed=0, transcendentals=0),
        name="mix",
    )(table, kind)


def spread_kernel(count, groups, mix_ref, *refs):
    out_ref, token_ref = refs[-2:]
    token_ref[...] = jnp.zeros_like(token_ref)
    experts, tile, width = out_ref.shape
    rows = jnp.concatenate([ref[...] for ref in refs[:count]], axis=0)
    rows = jnp.concatenate([rows, rows], axis=0)
    span = experts // groups
    for g in range(groups):
        part = jnp.dot(
            mix_ref[pl.ds(g * span * tile, span * tile), :], rows, preferred_element_type=jnp.float32
        )
        out_ref[pl.ds(g * span, span)] = part.astype(out_ref.dtype).reshape(span, tile, width)


def spread(mix, pieces, previous, experts, first, rows_all, tile):
    rows, width = pieces[0].shape
    count = len(pieces)
    groups = 4 if experts % 4 == 0 else 1
    specs = [pl.BlockSpec(mix.shape, lambda i: (0, 0))]
    specs += [pl.BlockSpec((tile, width), lambda i: (i, 0))] * count
    operands = [mix, *pieces]
    aliases = {}
    if previous is not None:
        specs.append(pl.BlockSpec(memory_space=pl.ANY))
        operands.append(previous)
        aliases = {len(operands) - 1: 0}
    return pl.pallas_call(
        functools.partial(spread_kernel, count, groups),
        grid=(rows // tile,),
        in_specs=specs,
        out_specs=[
            pl.BlockSpec((experts, tile, width), lambda i: (0, first // tile + i, 0)),
            pl.BlockSpec((8, 128), lambda i: (0, 0)),
        ],
        out_shape=[
            jax.ShapeDtypeStruct((experts, rows_all, width), jnp.bfloat16),
            jax.ShapeDtypeStruct((8, 128), jnp.float32),
        ],
        input_output_aliases=aliases,
        compiler_params=pltpu.CompilerParams(vmem_limit_bytes=16 << 20),
        cost_estimate=pl.CostEstimate(
            flops=2 * mix.size * rows // tile * width, bytes_accessed=2 * experts * rows * width, transcendentals=0
        ),
        name="spread",
    )(*operands)


def swaps(at, edge_size, sys_size):
    pairs = []
    for z in range(edge_size):
        other = z + 1 if (z - at) % 2 == 0 else z - 1
        for core in range(sys_size):
            if 0 <= other < edge_size:
                pairs.append((z * sys_size + core, other * sys_size + core))
            elif sys_size % 2 == 0:
                pairs.append((z * sys_size + core, z * sys_size + (core ^ 1)))
    return pairs


def shift(size, by):
    return [(i, (i + by) % size) for i in range(size)]


def body(edge_inputs, out_grad, expert_weights, coef_table, system_kind, edge_counts):
    edge_size = lax.axis_size("edge")
    expert_size = lax.axis_size("expert")
    sys_size = lax.axis_size("sys")
    exp_local, row_count, _ = expert_weights.shape
    width_in = edge_inputs.shape[2]
    edge_rows = out_grad.shape[1]
    chunks, rows, halves = layout(row_count)
    half = rows // 2
    tile = 32 if rows % 32 == 0 else 16
    features, grad = edge_inputs[0], out_grad[0]
    places = edge_size * chunks

    scale = 1.0 / math.sqrt(edge_rows * edge_size)
    mix = mix_matrix(coef_table, system_kind, expert_size, sys_size, exp_local, scale, tile)

    steps = plan(edge_size, chunks, halves)
    moves = [(at, part) for at, step in enumerate(steps) if step for part in parts_of(at, halves)]

    def extent(h, part):
        return (h * rows, rows) if part is None else (h * rows + part * half, half)

    def from_ends(at):
        far = all(b == (0 if source else edge_size - 1) for source, _, _, b, _, _ in steps[at])
        return far and all(kind == "S" and came is None for _, _, kind, _, _, came in steps[at])

    early = [(at, part) for at, part in moves if from_ends(at)]
    pieces = [extent(steps[at][0][4], part) for at, part in early]
    firsts = dict(zip(early, end_products(edge_counts, features, grad, sys_size, edge_size, row_count, pieces)))
    store, live = outer_products(edge_counts, features, grad, sys_size, (2 * places + 1) * rows)
    exchanged = []
    for h in range(chunks):
        parts = merge_part(
            coef_table, system_kind, expert_weights, expert_size, sys_size, h * rows, rows, tile
        )
        arrays = [parts[0]]
        arrays += [lax.ppermute(parts[k], "expert", shift(expert_size, k)) for k in range(1, expert_size)]
        exchanged.append(arrays)

    pending = []
    got = {}
    merged = set()
    waiting = {h: 2 * edge_size - 2 for h in range(chunks)}
    taken = set()
    result = None

    def own(first):
        return [first + z * row_count for z in range(edge_size)]

    def row_at(kind, b):
        return b * row_count + (width_in if kind == "M" else 0)

    def settle(store, move, origin, count, behind=()):
        at, part = move
        take, add = [2 * width_in] * edge_size, [0] * edge_size
        for _, target, kind, b, h, _ in steps[at]:
            take[target] = row_at(kind, b) + extent(h, part)[0]
            add[target] = int(kind == "S")
            if kind == "S" and b == target:
                waiting[h] -= 1 if part is None else 0.5
        pending.remove(move)
        return hop(store, [got.pop(move)], take, add, origin, count, behind)

    tokens = {}

    mixed = [mix]

    def overdue(at):
        late = [tokens.pop(h) for h in list(tokens) if at >= entry(SPREAD_BEFORE, h)]
        if mixed and at >= MIX_BEFORE:
            late.append(mixed.pop())
        return late

    def finish(store, result):
        for h in range(chunks):
            if waiting[h] or h in taken:
                continue
            taken.add(h)
            store, rows_h = hop(store, [], None, None, own(h * rows), rows)
            column = [rows_h]
            for k in range(1, expert_size):
                column.append(lax.ppermute(rows_h, "expert", shift(expert_size, k)))
            pieces = list(column)
            for l in range(1, sys_size):
                pieces += [lax.ppermute(piece, "sys", shift(sys_size, l)) for piece in column]
            result, token = spread(mix, pieces, result, exp_local, h * rows, row_count, tile)
            tokens[h] = token
        return store, result

    used = [at for at, step in enumerate(steps) if step]
    last, first_of_last = {}, used[-1]
    for at in reversed(used[-2:]):
        new = {target: b * chunks + h for _, target, kind, b, h, _ in steps[at] if kind == "M"}
        if set(new) & set(last):
            break
        last.update(new)
        first_of_last = at
    product = None

    def whole_product(store):
        return input_product(live, store, width_in)

    for move in moves:
        at, part = move
        step = steps[at]
        for source, _, kind, b, h, _ in step:
            if kind == "M" and b == source and h not in merged:
                merged.add(h)
                behind = [exchanged[1][0]] if chunks > 1 and MERGES_TOGETHER else []
                (store,) = hop(store, exchanged[h], own(width_in + h * rows), [0] * edge_size, None, rows, behind)
        origin, count, needed = [2 * width_in] * edge_size, None, set()
        for source, _, kind, b, h, came in step:
            first, count = extent(h, part)
            origin[source] = row_at(kind, b) + first
            if came is not None:
                brought = parts_of(came, halves)
                needed |= {(came, one) for one in brought if part is None or one is None or one == part}
        due = [one for one in pending if one in needed or one[0] <= at - LAG]
        for one in due:
            waits = one[0] >= first_of_last
            if waits and product is None:
                product = whole_product(store)
            behind = overdue(at) + ([product] if waits else [])
            if one == due[-1]:
                store, message = settle(store, one, origin, count, behind)
            else:
                (store,) = settle(store, one, None, rows, behind)
                store, result = finish(store, result)
        if move in firsts:
            message = firsts[move]
        elif not due:
            store, message = hop(store, [], None, None, origin, count, overdue(at))
        got[move] = lax.ppermute(message, ("edge", "sys"), swaps(at, edge_size, sys_size))
        pending.append(move)
        store, result = finish(store, result)
    while pending:
        waits = pending[0][0] >= first_of_last
        if waits and product is None:
            product = whole_product(store)
        behind = (list(tokens.values()) if len(pending) == 1 else []) + ([product] if waits else [])
        (store,) = settle(store, pending[0], None, rows, behind)
        store, result = finish(store, result)
    last = [last.get(z, 0) for z in range(edge_size)]
    input_grad = last_product(live, store, product, rows, last)
    return (input_grad[None], result)


def solution(mesh):
    specs = dict(
        mesh=mesh,
        in_specs=(
            P(("groups", "expert", "sys"), "edge", None),
            P(("groups", "expert", "sys"), "edge", None),
            P("expert", "edge", None),
            P(),
            P("groups"),
            P("groups"),
        ),
        out_specs=(
            P(("groups", "expert", "sys"), "edge", None),
            P(("groups", "expert"), "edge", None),
        ),
        check_vma=False,
    )

    def program(*args):
        return jax.shard_map(body, **specs)(*args)

    return program
```

```python
import functools
import math

import jax
import jax.numpy as jnp
from jax import lax
from jax.experimental import pallas as pl
from jax.experimental.pallas import tpu as pltpu
from jax.sharding import PartitionSpec as P


LAG, TAKEN_BY = 3, 4
SPLIT = ()
SKIPPED = (4,)
SUMS_FIRST, SUMS_CHUNK, ROWS_CHUNK, OWN_WEIGHT = 3, 1, 0, -0.7
MERGED_AT = (6, 8)
SPREAD_BEFORE = (17, 99)
MIX_BEFORE = 12
ENDS_GRANT = 62 << 20
MERGES_TOGETHER = True


def entry(values, at):
    return values[min(at, len(values) - 1)] + 4 * max(0, at - len(values) + 1)


def plan(size, chunks, halves):
    sums = {}
    rows = {}
    for h in range(chunks):
        for b in range(size):
            rows[b, b, h] = (entry(MERGED_AT, h), entry(MERGED_AT, h), None)
            if b > 0:
                sums[0, 1, b, h] = (0, 0, None)
            if b < size - 1:
                sums[size - 1, -1, b, h] = (0, 0, None)
    sent = set()
    steps = []
    total = 2 * chunks * size * (size - 1)
    while len(sent) < total:
        at = len(steps)
        step = []
        for low in range(at % 2, 0 if at in SKIPPED else size - 1, 2):
            for source, way in ((low, 1), (low + 1, -1)):
                target = source + way
                left = size - 1 - target if way == 1 else target
                ready = []
                for h in range(chunks):
                    for b in range(size):
                        ahead = (b - target) * way
                        own = OWN_WEIGHT if b == source else 0
                        for kind, state, order in (
                            ("S", sums.get((source, way, b, h)) if ahead >= 0 else None, SUMS_CHUNK * h - ahead - SUMS_FIRST),
                            ("M", rows.get((source, b, h)) if (source - b) * way >= 0 else None, ROWS_CHUNK * h - left + own),
                        ):
                            if state and state[0] <= at and (kind, source, way, b, h) not in sent:
                                ready.append(((state[1] > at, order, kind != "S", h), (kind, b, h), state[2]))
                if ready:
                    _, (kind, b, h), came = min(ready, key=lambda choice: choice[0])
                    sent.add((kind, source, way, b, h))
                    step.append((source, target, kind, b, h, came))
        lag = 1 if halves and at % 2 and at in SPLIT else LAG
        for source, target, kind, b, h, _ in step:
            if kind == "M":
                rows[target, b, h] = (at + lag, at + LAG, at)
            elif b != target:
                sums[target, target - source, b, h] = (at + lag, at + LAG, at)
        steps.append(step)
    return steps


def parts_of(at, halves):
    return (0, 1) if halves and at in SPLIT else (None,)


def layout(row_count):
    chunks = 2 if row_count % 32 == 0 else 1
    rows = row_count // chunks
    return chunks, rows, rows % 32 == 0


def at_device(values):
    place = lax.axis_index("edge")
    result = jnp.int32(values[0])
    for z in range(1, len(values)):
        if values[z] != values[z - 1]:
            result = jnp.where(place >= z, jnp.int32(values[z]), result)
    return result


def coefficient(table_ref, kind_ref, system, expert):
    return table_ref[kind_ref[system], expert]


def merge_kernel(expert_size, sys_size, first, table_ref, kind_ref, weights_ref, *out_refs):
    experts, _, width = weights_ref.shape
    rows = out_refs[0].shape[0]
    place = lax.axis_index("expert")
    core = lax.axis_index("sys")
    factors = [
        [
            coefficient(table_ref, kind_ref, lax.rem(place + k, expert_size) * sys_size + core, place * experts + e)
            for e in range(experts)
        ]
        for k in range(expert_size)
    ]

    lanes = 384 if width % 384 == 0 else width

    def step(i, _):
        for lane in range(0, width, lanes):
            columns = pl.ds(lane, lanes)
            here = pl.ds(pl.multiple_of(first + i * 16, 16), 16)
            totals = [None] * expert_size
            for e in range(experts):
                weight = weights_ref[e, here, columns].astype(jnp.float32)
                for k in range(expert_size):
                    term = factors[k][e] * weight
                    totals[k] = term if totals[k] is None else totals[k] + term
            for k in range(expert_size):
                out_refs[k][pl.ds(pl.multiple_of(i * 16, 16), 16), columns] = totals[k].astype(jnp.bfloat16)
        return 0

    lax.fori_loop(0, rows // 16, step, 0)


def merge_part(table, kind, weights, expert_size, sys_size, first, rows):
    experts, _, width = weights.shape
    return pl.pallas_call(
        functools.partial(merge_kernel, expert_size, sys_size, first),
        in_specs=[
            pl.BlockSpec(memory_space=pltpu.SMEM),
            pl.BlockSpec(memory_space=pltpu.SMEM),
            pl.BlockSpec(memory_space=pltpu.VMEM),
        ],
        out_specs=[pl.BlockSpec(memory_space=pltpu.VMEM)] * expert_size,
        out_shape=[jax.ShapeDtypeStruct((rows, width), jnp.bfloat16)] * expert_size,
        compiler_params=pltpu.CompilerParams(vmem_limit_bytes=8 << 20),
        cost_estimate=pl.CostEstimate(
            flops=2 * expert_size * experts * rows * width,
            bytes_accessed=2 * experts * rows * width,
            transcendentals=0,
        ),
        name="merge",
    )(table, kind, weights)


def live_rows(grad_ref, counts_ref, sys_size):
    system = lax.axis_index("expert") * sys_size + lax.axis_index("sys")
    live = counts_ref[system] - lax.axis_index("edge") * grad_ref.shape[0]
    at = lax.broadcasted_iota(jnp.int32, grad_ref.shape, 0)
    return jnp.where(at < live, grad_ref[...], jnp.zeros((), grad_ref.dtype))


def ends_kernel(sys_size, pieces, starts, span, counts_ref, features_ref, grad_ref, *refs):
    outs, (features, grad, product, ready) = refs[:-4], refs[-4:]
    lanes = features.shape[1]
    first = at_device(starts)
    window = pl.multiple_of(at_device([one // 128 * 128 if one + lanes <= span else span - lanes for one in starts]), 128)
    loads = [
        pltpu.make_async_copy(grad_ref, grad, ready.at[0]),
        pltpu.make_async_copy(features_ref.at[:, pl.ds(window, lanes)], features, ready.at[1]),
    ]
    for load in loads:
        load.start()
    for load in loads:
        load.wait()
    product[...] = lax.dot_general(
        features[...],
        live_rows(grad, counts_ref, sys_size),
        (((0,), (0,)), ((), ())),
        preferred_element_type=jnp.float32,
    ).astype(product.dtype)
    for (start, rows), out_ref in zip(pieces, outs):
        out_ref[...] = product[pl.ds(pl.multiple_of(first - window + start, 16), rows), :]


def end_products(counts, features, grad, sys_size, edge_size, block, pieces):
    edges, width_in = features.shape
    width = grad.shape[1]
    base = min(start for start, _ in pieces)
    extent = max(start + rows for start, rows in pieces) - base
    starts = [base + (0 if z else (edge_size - 1) * block) for z in range(edge_size)]
    lanes = min(width_in, max(-(-(one % 128 + extent) // 128) * 128 for one in starts))
    pieces = [(start - base, rows) for start, rows in pieces]
    return pl.pallas_call(
        functools.partial(ends_kernel, sys_size, pieces, starts, width_in),
        in_specs=[
            pl.BlockSpec(memory_space=pltpu.SMEM),
            pl.BlockSpec(memory_space=pl.ANY),
            pl.BlockSpec(memory_space=pl.ANY),
        ],
        out_specs=[pl.BlockSpec(memory_space=pltpu.VMEM)] * len(pieces),
        out_shape=[jax.ShapeDtypeStruct((rows, width), jnp.bfloat16) for _, rows in pieces],
        scratch_shapes=[
            pltpu.VMEM((edges, lanes), jnp.bfloat16),
            pltpu.VMEM((edges, width), jnp.bfloat16),
            pltpu.VMEM((lanes, width), jnp.bfloat16),
            pltpu.SemaphoreType.DMA((2,)),
        ],
        compiler_params=pltpu.CompilerParams(vmem_limit_bytes=ENDS_GRANT),
        cost_estimate=pl.CostEstimate(
            flops=2 * edges * lanes * width, bytes_accessed=2 * edges * (lanes + width), transcendentals=0
        ),
        name="ends",
    )(counts, features, grad)


def outer_kernel(sys_size, counts_ref, features_ref, grad_ref, out_ref, live_ref):
    @pl.when(pl.program_id(0) == 0)
    def _():
        live_ref[...] = live_rows(grad_ref, counts_ref, sys_size)

    out_ref[...] = lax.dot_general(
        features_ref[...], live_ref[...], (((0,), (0,)), ((), ())), preferred_element_type=jnp.float32
    ).astype(out_ref.dtype)


def outer_products(counts, features, grad, sys_size, store_rows):
    edges, width_in = features.shape
    width = grad.shape[1]
    tile = 256 if width_in % 256 == 0 else width_in
    return pl.pallas_call(
        functools.partial(outer_kernel, sys_size),
        grid=(width_in // tile,),
        in_specs=[
            pl.BlockSpec(memory_space=pltpu.SMEM),
            pl.BlockSpec((edges, tile), lambda i: (0, i)),
            pl.BlockSpec((edges, width), lambda i: (0, 0)),
        ],
        out_specs=[
            pl.BlockSpec((tile, width), lambda i: (i, 0)),
            pl.BlockSpec((edges, width), lambda i: (0, 0)),
        ],
        out_shape=[
            jax.ShapeDtypeStruct((store_rows, width), jnp.bfloat16),
            jax.ShapeDtypeStruct((edges, width), jnp.bfloat16),
        ],
        compiler_params=pltpu.CompilerParams(vmem_limit_bytes=12 << 20),
        cost_estimate=pl.CostEstimate(
            flops=2 * edges * width_in * width,
            bytes_accessed=2 * (edges * width_in + edges * width + width_in * width),
            transcendentals=0,
        ),
        name="outer",
    )(counts, features, grad)


def columns_kernel(width_in, firsts, live_ref, store_ref, *refs):
    out_ref, token_ref, part, done = refs[-4:]
    token_ref[...] = jnp.zeros_like(token_ref)
    count, _, tile = part.shape
    first = at_device(firsts)
    writes = []
    for t in range(count):
        columns = pl.ds(pl.multiple_of(first + t * tile, 128), tile)
        rows = pl.ds(pl.multiple_of(width_in + first + t * tile, 16), tile)
        part[t] = lax.dot_general(
            live_ref[...], store_ref[rows, :], (((1,), (1,)), ((), ())), preferred_element_type=jnp.float32
        ).astype(part.dtype)
        writes.append(pltpu.make_async_copy(part.at[t], out_ref.at[:, columns], done.at[t]))
        writes[-1].start()
    for write in writes:
        write.wait()


def columns(live, store, product, width_in, firsts, count, tile):
    edges, width = live.shape
    vmem = pl.BlockSpec(memory_space=pltpu.VMEM)
    keep = pl.BlockSpec(memory_space=pl.ANY)
    return pl.pallas_call(
        functools.partial(columns_kernel, width_in, firsts),
        in_specs=[vmem, vmem] + ([] if product is None else [keep]),
        out_specs=[keep, vmem],
        out_shape=[
            jax.ShapeDtypeStruct((edges, width_in), jnp.bfloat16),
            jax.ShapeDtypeStruct((8, 128), jnp.float32),
        ],
        input_output_aliases={} if product is None else {2: 0},
        scratch_shapes=[pltpu.VMEM((count, edges, tile), jnp.bfloat16), pltpu.SemaphoreType.DMA((count,))],
        compiler_params=pltpu.CompilerParams(vmem_limit_bytes=8 << 20),
        cost_estimate=pl.CostEstimate(
            flops=2 * edges * count * tile * width, bytes_accessed=2 * edges * count * tile, transcendentals=0
        ),
        name="columns",
    )(live, store, *([] if product is None else [product]))


def hop_kernel(count, behind, take, add, origin, *refs):
    arrays, (store, *message) = refs[1 : 1 + count], refs[1 + count + behind :]
    if count:
        into = at_device(take)
        adds = at_device(add) == 1

        def update(i, _):
            span = pl.ds(pl.multiple_of(i * 16, 16), 16)
            here = pl.ds(pl.multiple_of(into + i * 16, 16), 16)
            total = arrays[0][span, :].astype(jnp.float32)
            for ref in arrays[1:]:
                total = total + ref[span, :].astype(jnp.float32)
            total = jnp.where(adds, store[here, :].astype(jnp.float32) + total, total)
            store[here, :] = total.astype(store.dtype)
            return 0

        lax.fori_loop(0, arrays[0].shape[0] // 16, update, 0)
    if message:
        out = message[0]
        first = at_device(origin)

        def copy(i, _):
            span = pl.ds(pl.multiple_of(i * 16, 16), 16)
            out[span, :] = store[pl.ds(pl.multiple_of(first + i * 16, 16), 16), :]
            return 0

        lax.fori_loop(0, out.shape[0] // 16, copy, 0)


def hop(store, arrays, take, add, origin, rows, behind=()):
    width = store.shape[1]
    vmem = pl.BlockSpec(memory_space=pltpu.VMEM)
    shapes = [jax.ShapeDtypeStruct(store.shape, store.dtype)]
    if origin is not None:
        shapes.append(jax.ShapeDtypeStruct((rows, width), store.dtype))
    return pl.pallas_call(
        functools.partial(hop_kernel, len(arrays), len(behind), take, add, origin),
        in_specs=[vmem] * (1 + len(arrays)) + [pl.BlockSpec(memory_space=pl.ANY)] * len(behind),
        out_specs=[vmem] * len(shapes),
        out_shape=shapes,
        input_output_aliases={0: 0},
        compiler_params=pltpu.CompilerParams(vmem_limit_bytes=1 << 20),
        cost_estimate=pl.CostEstimate(flops=rows * width, bytes_accessed=4 * rows * width, transcendentals=0),
        name="hop",
    )(store, *arrays, *behind)


def mix_kernel(expert_size, sys_size, scale, tile, table_ref, kind_ref, out_ref):
    width = out_ref.shape[1]
    slots = expert_size * sys_size
    experts = out_ref.shape[0] // tile
    place = lax.axis_index("expert")
    core = lax.axis_index("sys")
    line = lax.broadcasted_iota(jnp.int32, (tile, width), 0)
    lane = lax.broadcasted_iota(jnp.int32, (tile, width), 1)
    upper = lane < slots * tile
    lane = jnp.where(upper, lane, lane - slots * tile)
    slot_at = lane // tile
    hit = (lane - slot_at * tile) == line
    systems = [
        lax.rem(place + expert_size - k, expert_size) * sys_size + lax.rem(core + sys_size - l, sys_size)
        for l in range(sys_size)
        for k in range(expert_size)
    ]
    for e in range(experts):
        value = jnp.zeros((tile, width), jnp.float32)
        for slot, system in enumerate(systems):
            factor = coefficient(table_ref, kind_ref, system, place * experts + e) * scale
            value = jnp.where(slot_at == slot, factor, value)
        high = value.astype(jnp.bfloat16)
        low = (value - high.astype(jnp.float32)).astype(jnp.bfloat16)
        value = jnp.where(upper, high.astype(jnp.float32), low.astype(jnp.float32))
        out_ref[pl.ds(e * tile, tile), :] = jnp.where(hit, value, 0.0).astype(jnp.bfloat16)


def mix_matrix(table, kind, expert_size, sys_size, experts, scale, tile):
    width = 2 * expert_size * sys_size * tile
    return pl.pallas_call(
        functools.partial(mix_kernel, expert_size, sys_size, scale, tile),
        in_specs=[pl.BlockSpec(memory_space=pltpu.SMEM)] * 2,
        out_specs=pl.BlockSpec(memory_space=pltpu.VMEM),
        out_shape=jax.ShapeDtypeStruct((experts * tile, width), jnp.bfloat16),
        compiler_params=pltpu.CompilerParams(vmem_limit_bytes=4 << 20),
        cost_estimate=pl.CostEstimate(flops=10 * experts * tile * width, bytes_accessed=0, transcendentals=0),
        name="mix",
    )(table, kind)


def spread_kernel(count, groups, mix_ref, *refs):
    out_ref, token_ref = refs[-2:]
    token_ref[...] = jnp.zeros_like(token_ref)
    experts, tile, width = out_ref.shape
    rows = jnp.concatenate([ref[...] for ref in refs[:count]], axis=0)
    rows = jnp.concatenate([rows, rows], axis=0)
    span = experts // groups
    for g in range(groups):
        part = jnp.dot(
            mix_ref[pl.ds(g * span * tile, span * tile), :], rows, preferred_element_type=jnp.float32
        )
        out_ref[pl.ds(g * span, span)] = part.astype(out_ref.dtype).reshape(span, tile, width)


def spread(mix, pieces, previous, experts, first, rows_all, tile):
    rows, width = pieces[0].shape
    count = len(pieces)
    groups = 4 if experts % 4 == 0 else 1
    specs = [pl.BlockSpec(mix.shape, lambda i: (0, 0))]
    specs += [pl.BlockSpec((tile, width), lambda i: (i, 0))] * count
    operands = [mix, *pieces]
    aliases = {}
    if previous is not None:
        specs.append(pl.BlockSpec(memory_space=pl.ANY))
        operands.append(previous)
        aliases = {len(operands) - 1: 0}
    return pl.pallas_call(
        functools.partial(spread_kernel, count, groups),
        grid=(rows // tile,),
        in_specs=specs,
        out_specs=[
            pl.BlockSpec((experts, tile, width), lambda i: (0, first // tile + i, 0)),
            pl.BlockSpec((8, 128), lambda i: (0, 0)),
        ],
        out_shape=[
            jax.ShapeDtypeStruct((experts, rows_all, width), jnp.bfloat16),
            jax.ShapeDtypeStruct((8, 128), jnp.float32),
        ],
        input_output_aliases=aliases,
        compiler_params=pltpu.CompilerParams(vmem_limit_bytes=16 << 20),
        cost_estimate=pl.CostEstimate(
            flops=2 * mix.size * rows // tile * width, bytes_accessed=2 * experts * rows * width, transcendentals=0
        ),
        name="spread",
    )(*operands)


def swaps(at, edge_size, sys_size):
    pairs = []
    for z in range(edge_size):
        other = z + 1 if (z - at) % 2 == 0 else z - 1
        for core in range(sys_size):
            if 0 <= other < edge_size:
                pairs.append((z * sys_size + core, other * sys_size + core))
            elif sys_size % 2 == 0:
                pairs.append((z * sys_size + core, z * sys_size + (core ^ 1)))
    return pairs


def shift(size, by):
    return [(i, (i + by) % size) for i in range(size)]


def body(edge_inputs, out_grad, expert_weights, coef_table, system_kind, edge_counts):
    edge_size = lax.axis_size("edge")
    expert_size = lax.axis_size("expert")
    sys_size = lax.axis_size("sys")
    exp_local, row_count, _ = expert_weights.shape
    width_in = edge_inputs.shape[2]
    edge_rows = out_grad.shape[1]
    chunks, rows, halves = layout(row_count)
    half = rows // 2
    tile = 32 if rows % 32 == 0 else 16
    features, grad = edge_inputs[0], out_grad[0]
    places = edge_size * chunks

    scale = 1.0 / math.sqrt(edge_rows * edge_size)
    mix = mix_matrix(coef_table, system_kind, expert_size, sys_size, exp_local, scale, tile)

    steps = plan(edge_size, chunks, halves)
    moves = [(at, part) for at, step in enumerate(steps) if step for part in parts_of(at, halves)]

    def extent(h, part):
        return (h * rows, rows) if part is None else (h * rows + part * half, half)

    def from_ends(at):
        far = all(b == (0 if source else edge_size - 1) for source, _, _, b, _, _ in steps[at])
        return far and all(kind == "S" and came is None for _, _, kind, _, _, came in steps[at])

    early = [(at, part) for at, part in moves if from_ends(at)]
    pieces = [extent(steps[at][0][4], part) for at, part in early]
    firsts = dict(zip(early, end_products(edge_counts, features, grad, sys_size, edge_size, row_count, pieces)))
    store, live = outer_products(edge_counts, features, grad, sys_size, (2 * places + 1) * rows)
    exchanged = []
    for h in range(chunks):
        parts = merge_part(coef_table, system_kind, expert_weights, expert_size, sys_size, h * rows, rows)
        arrays = [parts[0]]
        arrays += [lax.ppermute(parts[k], "expert", shift(expert_size, k)) for k in range(1, expert_size)]
        exchanged.append(arrays)

    pending = []
    got = {}
    merged = set()
    waiting = {h: 2 * edge_size - 2 for h in range(chunks)}
    taken = set()
    result = None

    def own(first):
        return [first + z * row_count for z in range(edge_size)]

    def row_at(kind, b):
        return b * row_count + (width_in if kind == "M" else 0)

    def settle(store, move, origin, count, behind=()):
        at, part = move
        take, add = [2 * width_in] * edge_size, [0] * edge_size
        for _, target, kind, b, h, _ in steps[at]:
            take[target] = row_at(kind, b) + extent(h, part)[0]
            add[target] = int(kind == "S")
            if kind == "S" and b == target:
                waiting[h] -= 1 if part is None else 0.5
        pending.remove(move)
        return hop(store, [got.pop(move)], take, add, origin, count, behind)

    tokens = {}

    mixed = [mix]

    def overdue(at):
        late = [tokens.pop(h) for h in list(tokens) if at >= entry(SPREAD_BEFORE, h)]
        if mixed and at >= MIX_BEFORE:
            late.append(mixed.pop())
        return late

    def finish(store, result):
        for h in range(chunks):
            if waiting[h] or h in taken:
                continue
            taken.add(h)
            store, rows_h = hop(store, [], None, None, own(h * rows), rows)
            column = [rows_h]
            for k in range(1, expert_size):
                column.append(lax.ppermute(rows_h, "expert", shift(expert_size, k)))
            pieces = list(column)
            for l in range(1, sys_size):
                pieces += [lax.ppermute(piece, "sys", shift(sys_size, l)) for piece in column]
            result, token = spread(mix, pieces, result, exp_local, h * rows, row_count, tile)
            tokens[h] = token
        return store, result

    def early_columns(settled):
        tiles, firsts = width_in // wide, []
        for z in range(edge_size):
            missing = [
                extent(h, part)[0] + b * row_count + r
                for at, part in moves
                if (at, part) not in settled
                for _, target, kind, b, h, _ in steps[at]
                if (target, kind) == (z, "M")
                for r in (0, extent(h, part)[1] - 1)
            ]
            low, high = min(missing, default=width_in), max(missing, default=0) + 1
            before, after = low // wide, (width_in - high) // wide
            tiles = min(tiles, max(before, after))
            firsts.append(before >= after)
        return tiles, [0 if first else width_in - tiles * wide for first in firsts]

    wide = 256 if width_in % 256 == 0 else width_in
    product, tiles, firsts_early = None, 0, [0] * edge_size
    for move in moves:
        at, part = move
        step = steps[at]
        for source, _, kind, b, h, _ in step:
            if kind == "M" and b == source and h not in merged:
                merged.add(h)
                behind = [exchanged[1][0]] if chunks > 1 and MERGES_TOGETHER else []
                (store,) = hop(store, exchanged[h], own(width_in + h * rows), [0] * edge_size, None, rows, behind)
        origin, count, needed = [2 * width_in] * edge_size, None, set()
        for source, _, kind, b, h, came in step:
            first, count = extent(h, part)
            origin[source] = row_at(kind, b) + first
            if came is not None:
                brought = parts_of(came, halves)
                needed |= {(came, one) for one in brought if part is None or one is None or one == part}
        due = [one for one in pending if one in needed or one[0] <= at - TAKEN_BY]
        for one in due:
            behind = overdue(at)
            if move == moves[-1] and one == due[-1]:
                tiles, firsts_early = early_columns([each for each in moves[:-1] if each not in pending])
                if tiles:
                    product, token = columns(live, store, None, width_in, firsts_early, tiles, wide)
                    behind.append(token)
            if one == due[-1]:
                store, message = settle(store, one, origin, count, behind)
            else:
                (store,) = settle(store, one, None, rows, behind)
                store, result = finish(store, result)
        if move in firsts:
            message = firsts[move]
        elif not due:
            store, message = hop(store, [], None, None, origin, count, overdue(at))
        got[move] = lax.ppermute(message, ("edge", "sys"), swaps(at, edge_size, sys_size))
        pending.append(move)
        store, result = finish(store, result)
    while pending:
        (store,) = settle(store, pending[0], None, rows, list(tokens.values()) if len(pending) == 1 else ())
        store, result = finish(store, result)
    rest = width_in // wide - tiles
    if rest:
        firsts_late = [0 if first else tiles * wide for first in firsts_early]
        product, _ = columns(live, store, product, width_in, firsts_late, rest, wide)
    return (product[None], result)


def solution(mesh):
    specs = dict(
        mesh=mesh,
        in_specs=(
            P(("groups", "expert", "sys"), "edge", None),
            P(("groups", "expert", "sys"), "edge", None),
            P("expert", "edge", None),
            P(),
            P("groups"),
            P("groups"),
        ),
        out_specs=(
            P(("groups", "expert", "sys"), "edge", None),
            P(("groups", "expert"), "edge", None),
        ),
        check_vma=False,
    )

    def program(*args):
        return jax.shard_map(body, **specs)(*args)

    return program
```

```python
import functools
import math

import jax
import jax.numpy as jnp
from jax import lax
from jax.experimental import pallas as pl
from jax.experimental.pallas import tpu as pltpu
from jax.sharding import PartitionSpec as P


LAG, TAKEN_BY = 3, 4
SPLIT = ()
SKIPPED = (4,)
SUMS_FIRST, SUMS_CHUNK, ROWS_CHUNK, OWN_WEIGHT = 3, 1, 0, -0.7
MERGED_AT = (6, 8)
SPREAD_BEFORE = (15, 99)
MIX_BEFORE = 12
ENDS_GRANT = 62 << 20
MERGES_TOGETHER = True


def entry(values, at):
    return values[min(at, len(values) - 1)] + 4 * max(0, at - len(values) + 1)


def plan(size, chunks, halves):
    sums = {}
    rows = {}
    for h in range(chunks):
        for b in range(size):
            rows[b, b, h] = (entry(MERGED_AT, h), entry(MERGED_AT, h), None)
            if b > 0:
                sums[0, 1, b, h] = (0, 0, None)
            if b < size - 1:
                sums[size - 1, -1, b, h] = (0, 0, None)
    sent = set()
    steps = []
    total = 2 * chunks * size * (size - 1)
    while len(sent) < total:
        at = len(steps)
        step = []
        for low in range(at % 2, 0 if at in SKIPPED else size - 1, 2):
            for source, way in ((low, 1), (low + 1, -1)):
                target = source + way
                left = size - 1 - target if way == 1 else target
                ready = []
                for h in range(chunks):
                    for b in range(size):
                        ahead = (b - target) * way
                        own = OWN_WEIGHT if b == source else 0
                        for kind, state, order in (
                            ("S", sums.get((source, way, b, h)) if ahead >= 0 else None, SUMS_CHUNK * h - ahead - SUMS_FIRST),
                            ("M", rows.get((source, b, h)) if (source - b) * way >= 0 else None, ROWS_CHUNK * h - left + own),
                        ):
                            if state and state[0] <= at and (kind, source, way, b, h) not in sent:
                                ready.append(((state[1] > at, order, kind != "S", h), (kind, b, h), state[2]))
                if ready:
                    _, (kind, b, h), came = min(ready, key=lambda choice: choice[0])
                    sent.add((kind, source, way, b, h))
                    step.append((source, target, kind, b, h, came))
        lag = 1 if halves and at % 2 and at in SPLIT else LAG
        for source, target, kind, b, h, _ in step:
            if kind == "M":
                rows[target, b, h] = (at + lag, at + LAG, at)
            elif b != target:
                sums[target, target - source, b, h] = (at + lag, at + LAG, at)
        steps.append(step)
    return steps


def parts_of(at, halves):
    return (0, 1) if halves and at in SPLIT else (None,)


def layout(row_count):
    chunks = 2 if row_count % 32 == 0 else 1
    rows = row_count // chunks
    return chunks, rows, rows % 32 == 0


def at_device(values):
    place = lax.axis_index("edge")
    result = jnp.int32(values[0])
    for z in range(1, len(values)):
        if values[z] != values[z - 1]:
            result = jnp.where(place >= z, jnp.int32(values[z]), result)
    return result


def coefficient(table_ref, kind_ref, system, expert):
    return table_ref[kind_ref[system], expert]


def merge_kernel(expert_size, sys_size, first, table_ref, kind_ref, weights_ref, *out_refs):
    experts, _, width = weights_ref.shape
    rows = out_refs[0].shape[0]
    place = lax.axis_index("expert")
    core = lax.axis_index("sys")
    factors = [
        [
            coefficient(table_ref, kind_ref, lax.rem(place + k, expert_size) * sys_size + core, place * experts + e)
            for e in range(experts)
        ]
        for k in range(expert_size)
    ]

    lanes = 384 if width % 384 == 0 else width

    def step(i, _):
        for lane in range(0, width, lanes):
            columns = pl.ds(lane, lanes)
            here = pl.ds(pl.multiple_of(first + i * 16, 16), 16)
            totals = [None] * expert_size
            for e in range(experts):
                weight = weights_ref[e, here, columns].astype(jnp.float32)
                for k in range(expert_size):
                    term = factors[k][e] * weight
                    totals[k] = term if totals[k] is None else totals[k] + term
            for k in range(expert_size):
                out_refs[k][pl.ds(pl.multiple_of(i * 16, 16), 16), columns] = totals[k].astype(jnp.bfloat16)
        return 0

    lax.fori_loop(0, rows // 16, step, 0)


def merge_part(table, kind, weights, expert_size, sys_size, first, rows):
    experts, _, width = weights.shape
    return pl.pallas_call(
        functools.partial(merge_kernel, expert_size, sys_size, first),
        in_specs=[
            pl.BlockSpec(memory_space=pltpu.SMEM),
            pl.BlockSpec(memory_space=pltpu.SMEM),
            pl.BlockSpec(memory_space=pltpu.VMEM),
        ],
        out_specs=[pl.BlockSpec(memory_space=pltpu.VMEM)] * expert_size,
        out_shape=[jax.ShapeDtypeStruct((rows, width), jnp.bfloat16)] * expert_size,
        compiler_params=pltpu.CompilerParams(vmem_limit_bytes=8 << 20),
        cost_estimate=pl.CostEstimate(
            flops=2 * expert_size * experts * rows * width,
            bytes_accessed=2 * experts * rows * width,
            transcendentals=0,
        ),
        name="merge",
    )(table, kind, weights)


def live_rows(grad_ref, counts_ref, sys_size):
    system = lax.axis_index("expert") * sys_size + lax.axis_index("sys")
    live = counts_ref[system] - lax.axis_index("edge") * grad_ref.shape[0]
    at = lax.broadcasted_iota(jnp.int32, grad_ref.shape, 0)
    return jnp.where(at < live, grad_ref[...], jnp.zeros((), grad_ref.dtype))


def ends_kernel(sys_size, pieces, starts, span, counts_ref, features_ref, grad_ref, *refs):
    outs, (features, grad, product, ready) = refs[:-4], refs[-4:]
    lanes = features.shape[1]
    first = at_device(starts)
    window = pl.multiple_of(at_device([one // 128 * 128 if one + lanes <= span else span - lanes for one in starts]), 128)
    loads = [
        pltpu.make_async_copy(grad_ref, grad, ready.at[0]),
        pltpu.make_async_copy(features_ref.at[:, pl.ds(window, lanes)], features, ready.at[1]),
    ]
    for load in loads:
        load.start()
    for load in loads:
        load.wait()
    product[...] = lax.dot_general(
        features[...],
        live_rows(grad, counts_ref, sys_size),
        (((0,), (0,)), ((), ())),
        preferred_element_type=jnp.float32,
    ).astype(product.dtype)
    for (start, rows), out_ref in zip(pieces, outs):
        out_ref[...] = product[pl.ds(pl.multiple_of(first - window + start, 16), rows), :]


def end_products(counts, features, grad, sys_size, edge_size, block, pieces):
    edges, width_in = features.shape
    width = grad.shape[1]
    base = min(start for start, _ in pieces)
    extent = max(start + rows for start, rows in pieces) - base
    starts = [base + (0 if z else (edge_size - 1) * block) for z in range(edge_size)]
    lanes = min(width_in, max(-(-(one % 128 + extent) // 128) * 128 for one in starts))
    pieces = [(start - base, rows) for start, rows in pieces]
    return pl.pallas_call(
        functools.partial(ends_kernel, sys_size, pieces, starts, width_in),
        in_specs=[
            pl.BlockSpec(memory_space=pltpu.SMEM),
            pl.BlockSpec(memory_space=pl.ANY),
            pl.BlockSpec(memory_space=pl.ANY),
        ],
        out_specs=[pl.BlockSpec(memory_space=pltpu.VMEM)] * len(pieces),
        out_shape=[jax.ShapeDtypeStruct((rows, width), jnp.bfloat16) for _, rows in pieces],
        scratch_shapes=[
            pltpu.VMEM((edges, lanes), jnp.bfloat16),
            pltpu.VMEM((edges, width), jnp.bfloat16),
            pltpu.VMEM((lanes, width), jnp.bfloat16),
            pltpu.SemaphoreType.DMA((2,)),
        ],
        compiler_params=pltpu.CompilerParams(vmem_limit_bytes=ENDS_GRANT),
        cost_estimate=pl.CostEstimate(
            flops=2 * edges * lanes * width, bytes_accessed=2 * edges * (lanes + width), transcendentals=0
        ),
        name="ends",
    )(counts, features, grad)


def outer_kernel(sys_size, counts_ref, features_ref, grad_ref, out_ref, live_ref):
    @pl.when(pl.program_id(0) == 0)
    def _():
        live_ref[...] = live_rows(grad_ref, counts_ref, sys_size)

    out_ref[...] = lax.dot_general(
        features_ref[...], live_ref[...], (((0,), (0,)), ((), ())), preferred_element_type=jnp.float32
    ).astype(out_ref.dtype)


def outer_products(counts, features, grad, sys_size, store_rows):
    edges, width_in = features.shape
    width = grad.shape[1]
    tile = 256 if width_in % 256 == 0 else width_in
    return pl.pallas_call(
        functools.partial(outer_kernel, sys_size),
        grid=(width_in // tile,),
        in_specs=[
            pl.BlockSpec(memory_space=pltpu.SMEM),
            pl.BlockSpec((edges, tile), lambda i: (0, i)),
            pl.BlockSpec((edges, width), lambda i: (0, 0)),
        ],
        out_specs=[
            pl.BlockSpec((tile, width), lambda i: (i, 0)),
            pl.BlockSpec((edges, width), lambda i: (0, 0)),
        ],
        out_shape=[
            jax.ShapeDtypeStruct((store_rows, width), jnp.bfloat16),
            jax.ShapeDtypeStruct((edges, width), jnp.bfloat16),
        ],
        compiler_params=pltpu.CompilerParams(vmem_limit_bytes=12 << 20),
        cost_estimate=pl.CostEstimate(
            flops=2 * edges * width_in * width,
            bytes_accessed=2 * (edges * width_in + edges * width + width_in * width),
            transcendentals=0,
        ),
        name="outer",
    )(counts, features, grad)


def columns_kernel(width_in, firsts, aliased, live_ref, store_ref, *refs):
    *outs, part, done = refs[aliased:]
    out_ref = outs[0]
    for token_ref in outs[1:]:
        token_ref[...] = jnp.zeros_like(token_ref)
    count, _, tile = part.shape
    first = at_device(firsts)
    writes = []
    for t in range(count):
        columns = pl.ds(pl.multiple_of(first + t * tile, 128), tile)
        rows = pl.ds(pl.multiple_of(width_in + first + t * tile, 16), tile)
        part[t] = lax.dot_general(
            live_ref[...], store_ref[rows, :], (((1,), (1,)), ((), ())), preferred_element_type=jnp.float32
        ).astype(part.dtype)
        writes.append(pltpu.make_async_copy(part.at[t], out_ref.at[:, columns], done.at[t]))
        writes[-1].start()
    for write in writes:
        write.wait()


def columns(live, store, product, width_in, firsts, count, tile, token=True):
    edges, width = live.shape
    vmem = pl.BlockSpec(memory_space=pltpu.VMEM)
    keep = pl.BlockSpec(memory_space=pl.ANY)
    return pl.pallas_call(
        functools.partial(columns_kernel, width_in, firsts, int(product is not None)),
        in_specs=[vmem, vmem] + ([] if product is None else [keep]),
        out_specs=[keep, vmem][: 1 + token],
        out_shape=[
            jax.ShapeDtypeStruct((edges, width_in), jnp.bfloat16),
            jax.ShapeDtypeStruct((8, 128), jnp.float32),
        ][: 1 + token],
        input_output_aliases={} if product is None else {2: 0},
        scratch_shapes=[pltpu.VMEM((count, edges, tile), jnp.bfloat16), pltpu.SemaphoreType.DMA((count,))],
        compiler_params=pltpu.CompilerParams(vmem_limit_bytes=8 << 20),
        cost_estimate=pl.CostEstimate(
            flops=2 * edges * count * tile * width, bytes_accessed=2 * edges * count * tile, transcendentals=0
        ),
        name="columns",
    )(live, store, *([] if product is None else [product]))


def hop_kernel(count, behind, take, add, origin, *refs):
    arrays, (store, *message) = refs[1 : 1 + count], refs[1 + count + behind :]
    if count:
        into = at_device(take)
        adds = at_device(add) == 1

        def update(i, _):
            span = pl.ds(pl.multiple_of(i * 16, 16), 16)
            here = pl.ds(pl.multiple_of(into + i * 16, 16), 16)
            total = arrays[0][span, :].astype(jnp.float32)
            for ref in arrays[1:]:
                total = total + ref[span, :].astype(jnp.float32)
            total = jnp.where(adds, store[here, :].astype(jnp.float32) + total, total)
            store[here, :] = total.astype(store.dtype)
            return 0

        lax.fori_loop(0, arrays[0].shape[0] // 16, update, 0)
    if message:
        out = message[0]
        first = at_device(origin)

        def copy(i, _):
            span = pl.ds(pl.multiple_of(i * 16, 16), 16)
            out[span, :] = store[pl.ds(pl.multiple_of(first + i * 16, 16), 16), :]
            return 0

        lax.fori_loop(0, out.shape[0] // 16, copy, 0)


def hop(store, arrays, take, add, origin, rows, behind=()):
    width = store.shape[1]
    vmem = pl.BlockSpec(memory_space=pltpu.VMEM)
    shapes = [jax.ShapeDtypeStruct(store.shape, store.dtype)]
    if origin is not None:
        shapes.append(jax.ShapeDtypeStruct((rows, width), store.dtype))
    return pl.pallas_call(
        functools.partial(hop_kernel, len(arrays), len(behind), take, add, origin),
        in_specs=[vmem] * (1 + len(arrays)) + [pl.BlockSpec(memory_space=pl.ANY)] * len(behind),
        out_specs=[vmem] * len(shapes),
        out_shape=shapes,
        input_output_aliases={0: 0},
        compiler_params=pltpu.CompilerParams(vmem_limit_bytes=1 << 20),
        cost_estimate=pl.CostEstimate(flops=rows * width, bytes_accessed=4 * rows * width, transcendentals=0),
        name="hop",
    )(store, *arrays, *behind)


def mix_kernel(expert_size, sys_size, scale, tile, table_ref, kind_ref, out_ref):
    width = out_ref.shape[1]
    slots = expert_size * sys_size
    experts = out_ref.shape[0] // tile
    place = lax.axis_index("expert")
    core = lax.axis_index("sys")
    line = lax.broadcasted_iota(jnp.int32, (tile, width), 0)
    lane = lax.broadcasted_iota(jnp.int32, (tile, width), 1)
    upper = lane < slots * tile
    lane = jnp.where(upper, lane, lane - slots * tile)
    slot_at = lane // tile
    hit = (lane - slot_at * tile) == line
    systems = [
        lax.rem(place + expert_size - k, expert_size) * sys_size + lax.rem(core + sys_size - l, sys_size)
        for l in range(sys_size)
        for k in range(expert_size)
    ]
    for e in range(experts):
        value = jnp.zeros((tile, width), jnp.float32)
        for slot, system in enumerate(systems):
            factor = coefficient(table_ref, kind_ref, system, place * experts + e) * scale
            value = jnp.where(slot_at == slot, factor, value)
        high = value.astype(jnp.bfloat16)
        low = (value - high.astype(jnp.float32)).astype(jnp.bfloat16)
        value = jnp.where(upper, high.astype(jnp.float32), low.astype(jnp.float32))
        out_ref[pl.ds(e * tile, tile), :] = jnp.where(hit, value, 0.0).astype(jnp.bfloat16)


def mix_matrix(table, kind, expert_size, sys_size, experts, scale, tile):
    width = 2 * expert_size * sys_size * tile
    return pl.pallas_call(
        functools.partial(mix_kernel, expert_size, sys_size, scale, tile),
        in_specs=[pl.BlockSpec(memory_space=pltpu.SMEM)] * 2,
        out_specs=pl.BlockSpec(memory_space=pltpu.VMEM),
        out_shape=jax.ShapeDtypeStruct((experts * tile, width), jnp.bfloat16),
        compiler_params=pltpu.CompilerParams(vmem_limit_bytes=4 << 20),
        cost_estimate=pl.CostEstimate(flops=10 * experts * tile * width, bytes_accessed=0, transcendentals=0),
        name="mix",
    )(table, kind)


def spread_kernel(count, groups, mix_ref, *refs):
    out_ref, token_ref = refs[-2:]
    token_ref[...] = jnp.zeros_like(token_ref)
    experts, tile, width = out_ref.shape
    rows = jnp.concatenate([ref[...] for ref in refs[:count]], axis=0)
    rows = jnp.concatenate([rows, rows], axis=0)
    span = experts // groups
    for g in range(groups):
        part = jnp.dot(
            mix_ref[pl.ds(g * span * tile, span * tile), :], rows, preferred_element_type=jnp.float32
        )
        out_ref[pl.ds(g * span, span)] = part.astype(out_ref.dtype).reshape(span, tile, width)


def spread(mix, pieces, previous, experts, first, rows_all, tile):
    rows, width = pieces[0].shape
    count = len(pieces)
    groups = 4 if experts % 4 == 0 else 1
    specs = [pl.BlockSpec(mix.shape, lambda i: (0, 0))]
    specs += [pl.BlockSpec((tile, width), lambda i: (i, 0))] * count
    operands = [mix, *pieces]
    aliases = {}
    if previous is not None:
        specs.append(pl.BlockSpec(memory_space=pl.ANY))
        operands.append(previous)
        aliases = {len(operands) - 1: 0}
    return pl.pallas_call(
        functools.partial(spread_kernel, count, groups),
        grid=(rows // tile,),
        in_specs=specs,
        out_specs=[
            pl.BlockSpec((experts, tile, width), lambda i: (0, first // tile + i, 0)),
            pl.BlockSpec((8, 128), lambda i: (0, 0)),
        ],
        out_shape=[
            jax.ShapeDtypeStruct((experts, rows_all, width), jnp.bfloat16),
            jax.ShapeDtypeStruct((8, 128), jnp.float32),
        ],
        input_output_aliases=aliases,
        compiler_params=pltpu.CompilerParams(vmem_limit_bytes=16 << 20),
        cost_estimate=pl.CostEstimate(
            flops=2 * mix.size * rows // tile * width, bytes_accessed=2 * experts * rows * width, transcendentals=0
        ),
        name="spread",
    )(*operands)


def swaps(at, edge_size, sys_size):
    pairs = []
    for z in range(edge_size):
        other = z + 1 if (z - at) % 2 == 0 else z - 1
        for core in range(sys_size):
            if 0 <= other < edge_size:
                pairs.append((z * sys_size + core, other * sys_size + core))
            elif sys_size % 2 == 0:
                pairs.append((z * sys_size + core, z * sys_size + (core ^ 1)))
    return pairs


def shift(size, by):
    return [(i, (i + by) % size) for i in range(size)]


def body(edge_inputs, out_grad, expert_weights, coef_table, system_kind, edge_counts):
    edge_size = lax.axis_size("edge")
    expert_size = lax.axis_size("expert")
    sys_size = lax.axis_size("sys")
    exp_local, row_count, _ = expert_weights.shape
    width_in = edge_inputs.shape[2]
    edge_rows = out_grad.shape[1]
    chunks, rows, halves = layout(row_count)
    half = rows // 2
    tile = 32 if rows % 32 == 0 else 16
    features, grad = edge_inputs[0], out_grad[0]
    places = edge_size * chunks

    scale = 1.0 / math.sqrt(edge_rows * edge_size)
    mix = mix_matrix(coef_table, system_kind, expert_size, sys_size, exp_local, scale, tile)

    steps = plan(edge_size, chunks, halves)
    moves = [(at, part) for at, step in enumerate(steps) if step for part in parts_of(at, halves)]

    def extent(h, part):
        return (h * rows, rows) if part is None else (h * rows + part * half, half)

    def from_ends(at):
        far = all(b == (0 if source else edge_size - 1) for source, _, _, b, _, _ in steps[at])
        return far and all(kind == "S" and came is None for _, _, kind, _, _, came in steps[at])

    early = [(at, part) for at, part in moves if from_ends(at)]
    pieces = [extent(steps[at][0][4], part) for at, part in early]
    firsts = dict(zip(early, end_products(edge_counts, features, grad, sys_size, edge_size, row_count, pieces)))
    store, live = outer_products(edge_counts, features, grad, sys_size, (2 * places + 1) * rows)
    exchanged = []
    for h in range(chunks):
        parts = merge_part(coef_table, system_kind, expert_weights, expert_size, sys_size, h * rows, rows)
        arrays = [parts[0]]
        arrays += [lax.ppermute(parts[k], "expert", shift(expert_size, k)) for k in range(1, expert_size)]
        exchanged.append(arrays)

    pending = []
    got = {}
    merged = set()
    waiting = {h: 2 * edge_size - 2 for h in range(chunks)}
    taken = set()
    result = None

    def own(first):
        return [first + z * row_count for z in range(edge_size)]

    def row_at(kind, b):
        return b * row_count + (width_in if kind == "M" else 0)

    def settle(store, move, origin, count, behind=()):
        at, part = move
        take, add = [2 * width_in] * edge_size, [0] * edge_size
        for _, target, kind, b, h, _ in steps[at]:
            take[target] = row_at(kind, b) + extent(h, part)[0]
            add[target] = int(kind == "S")
            if kind == "S" and b == target:
                waiting[h] -= 1 if part is None else 0.5
        pending.remove(move)
        return hop(store, [got.pop(move)], take, add, origin, count, behind)

    tokens = {}

    mixed = [mix]

    def overdue(at):
        late = [tokens.pop(h) for h in list(tokens) if at >= entry(SPREAD_BEFORE, h)]
        if mixed and at >= MIX_BEFORE:
            late.append(mixed.pop())
        return late

    def finish(store, result):
        for h in range(chunks):
            if waiting[h] or h in taken:
                continue
            taken.add(h)
            store, rows_h = hop(store, [], None, None, own(h * rows), rows)
            column = [rows_h]
            for k in range(1, expert_size):
                column.append(lax.ppermute(rows_h, "expert", shift(expert_size, k)))
            pieces = list(column)
            for l in range(1, sys_size):
                pieces += [lax.ppermute(piece, "sys", shift(sys_size, l)) for piece in column]
            result, token = spread(mix, pieces, result, exp_local, h * rows, row_count, tile)
            tokens[h] = token
        return store, result

    def early_columns(settled):
        tiles, firsts = width_in // wide, []
        for z in range(edge_size):
            missing = [
                extent(h, part)[0] + b * row_count + r
                for at, part in moves
                if (at, part) not in settled
                for _, target, kind, b, h, _ in steps[at]
                if (target, kind) == (z, "M")
                for r in (0, extent(h, part)[1] - 1)
            ]
            low, high = min(missing, default=width_in), max(missing, default=0) + 1
            before, after = low // wide, (width_in - high) // wide
            tiles = min(tiles, max(before, after))
            firsts.append(before >= after)
        return tiles, [0 if first else width_in - tiles * wide for first in firsts]

    wide = 256 if width_in % 256 == 0 else width_in
    product, tiles, firsts_early = None, 0, [0] * edge_size
    for move in moves:
        at, part = move
        step = steps[at]
        for source, _, kind, b, h, _ in step:
            if kind == "M" and b == source and h not in merged:
                merged.add(h)
                behind = [exchanged[1][0]] if chunks > 1 and MERGES_TOGETHER else []
                (store,) = hop(store, exchanged[h], own(width_in + h * rows), [0] * edge_size, None, rows, behind)
        origin, count, needed = [2 * width_in] * edge_size, None, set()
        for source, _, kind, b, h, came in step:
            first, count = extent(h, part)
            origin[source] = row_at(kind, b) + first
            if came is not None:
                brought = parts_of(came, halves)
                needed |= {(came, one) for one in brought if part is None or one is None or one == part}
        due = [one for one in pending if one in needed or one[0] <= at - TAKEN_BY]
        for one in due:
            behind = overdue(at)
            if move == moves[-1] and one == due[-1]:
                tiles, firsts_early = early_columns([each for each in moves[:-1] if each not in pending])
                if tiles:
                    product, token = columns(live, store, None, width_in, firsts_early, tiles, wide)
                    behind.append(token)
            if one == due[-1]:
                store, message = settle(store, one, origin, count, behind)
            else:
                (store,) = settle(store, one, None, rows, behind)
                store, result = finish(store, result)
        if move in firsts:
            message = firsts[move]
        elif not due:
            store, message = hop(store, [], None, None, origin, count, overdue(at))
        got[move] = lax.ppermute(message, ("edge", "sys"), swaps(at, edge_size, sys_size))
        pending.append(move)
        store, result = finish(store, result)
    while len(pending) > 1:
        (store,) = settle(store, pending[0], None, rows)
        store, result = finish(store, result)
    rest, behind = width_in // wide - tiles, []
    if rest:
        firsts_rest = [0 if first else tiles * wide for first in firsts_early]
        product, token = columns(live, store, product, width_in, firsts_rest, rest, wide)
        behind.append(token)
    last = [0] * edge_size
    at, part = pending[0]
    for _, target, kind, b, h, _ in steps[at]:
        if kind == "M":
            last[target] = b * row_count + extent(h, part)[0]
    span = min(width_in, max(-(-(first % 128 + extent(0, part)[1]) // 128) * 128 for first in last))
    firsts_last = [min(first // 128 * 128, width_in - span) for first in last]
    (store,) = settle(store, pending[0], None, rows, behind + list(tokens.values()))
    store, result = finish(store, result)
    (product,) = columns(live, store, product, width_in, firsts_last, 1, span, token=False)
    return (product[None], result)


def solution(mesh):
    specs = dict(
        mesh=mesh,
        in_specs=(
            P(("groups", "expert", "sys"), "edge", None),
            P(("groups", "expert", "sys"), "edge", None),
            P("expert", "edge", None),
            P(),
            P("groups"),
            P("groups"),
        ),
        out_specs=(
            P(("groups", "expert", "sys"), "edge", None),
            P(("groups", "expert"), "edge", None),
        ),
        check_vma=False,
    )

    def program(*args):
        return jax.shard_map(body, **specs)(*args)

    return program
```
